32 devices in a mesh: patch: 2 (over y), exp: 4 (over z), tile: 2 (over x), band: 2 (over core).
Axes of the slice: x: 2, y: 2, z: 4, core: 2. Of those that a mesh axis runs over, the one named last changes fastest.
Arguments:
- images: bfloat16 [4, 2, 64, 128, 128], P(('patch', 'band'), 'tile', 'exp'), parts along dimension 0, may hold values from -6 to 6
- mask_bits: int32 [4, 2, 64, 128, 128], P(('patch', 'band'), 'tile', 'exp'), parts along dimension 0, may hold values from 0 to 7
- inv_var: float32 [4, 2, 64], P(('patch', 'band'), 'tile', 'exp'), parts along dimension 0, may hold values from 0.5 to 4
- routes: int32 [4, 2, 64, 1], P(('patch', 'band'), 'tile', 'exp'), parts along dimension 0, may hold values from 0 to 3; in each aligned block of 16 rows (0 to 15, 16 to 31, ..., all dimensions but the last counted through in order) at most 8 rows name the same one
- block_slot: int32 [4, 2, 64], P(('patch', 'band'), 'tile', 'exp'), parts along dimension 0, may hold values from 0 to 7
- kernel_index: int32 [4, 2, 64], P(('patch', 'band'), 'tile', 'exp'), parts along dimension 0, may hold values from 0 to 63
- coefficients: float32 [64, 3], replicated, may hold values from -4 to 4
Outputs:
- coadd: float32 [4, 512, 2048], P(('patch', 'band'), 'tile', 'exp'), parts along dimension 0
- detection: float32 [1024, 2048], P(('patch', 'tile'), 'exp'), parts along dimension 0
The draws below stay inside these ranges and needn't reach their ends.
There are 2 independent parts, one for each index of `patch`. The reference program is written for one: setup_inputs(seed, part) draws one part's arguments, and reference() takes and returns one part's arrays. A program takes and returns all parts, laid end to end along the dimension named above; an argument that names none is the same for every part. Nothing has to cross between parts.
Inputs may be any that keep to these rules, and one draw needn't show every extreme that they name: Among the 16 sub-blocks of one device for one band and strip (an aligned block of routes), no tile column is named more than 8 times, and some tile column is named exactly 8 times.
All inputs are finite; a program needn't handle non-finite values.
Results may differ from the reference program's by a relative error of at most 0.0039.
Values may be sent and summed in bfloat16 or wider, within the bound.
A program may use at most 128 MiB of HBM per device.

```python
import math
import jax
import jax.numpy as jnp
import numpy as np
from jax import lax

BLOCK = 128
TAPS = 41
NCOEF = 64
SB = 16
BLOCK_ROWS = 2
BLOCK_COLS = 4
CAP = 8
SUBS = 64
STRIPS = 2
BANDS = 2
N_EXP = 4


def touch_ends(values, own_key, low, top_value):
    extent = values.shape
    index_at = [jax.random.randint(jax.random.fold_in(own_key, axis), (), 0, extent[axis]) for axis in range(len(extent))]
    values = values.at[tuple(index_at)].set(low)
    longest = extent.index(max(extent))
    index_at[longest] = (index_at[longest] + 1) % extent[longest]
    return values.at[tuple(index_at)].set(top_value)


def levels(stream_key, shape, shards, least, largest):
    loudness = 1.0
    for dim, blocks in shards:
        draws = jax.random.uniform(jax.random.fold_in(jax.random.fold_in(stream_key, 6), dim), (blocks,), jnp.float32, least / len(shards), largest / len(shards))
        loudness = loudness * jnp.repeat(jnp.exp(draws), shape[dim] // blocks).reshape((-1,) + (1,) * (len(shape) - 1 - dim))
    return loudness


def routed_block(own_key, own, number, rows, amount, top, limit, skew):
    ranking = jax.random.permutation(own_key, amount)
    packed, common = load_shares(amount, rows * top, limit, skew, True), load_shares(amount, rows * top, limit, skew, False)
    places = jnp.arange(amount)

    def named(lengths, offset_by):
        used = int((lengths > 0).sum())
        fixed = max(1, used // 4)
        moved = fixed + (places - fixed + offset_by * (used - fixed)) % max(1, amount - fixed)
        return jnp.zeros((amount,), jnp.int32).at[ranking[jnp.where(places < fixed, places, moved)]].set(jnp.asarray(lengths, jnp.int32))

    lengths = jnp.where(number % 4 == 0, named(packed, number // 4), named(common, number - number // 4 - 1))
    mixed = jax.random.permutation(jax.random.fold_in(own, 3), amount)
    source_of, taker = mixed[0:amount // 2 * 2:2], mixed[1:amount // 2 * 2:2]
    slack = jnp.minimum(lengths[source_of] - 1, limit - lengths[taker]) // 2
    slack = jnp.where((source_of == ranking[0]) | (taker == ranking[0]) | (lengths[taker] == 0), 0, jnp.maximum(slack, 0))
    moved = jax.random.randint(jax.random.fold_in(own, 4), (amount // 2,), 0, 1 << 20) % (slack + 1)
    lengths = lengths.at[source_of].add(-moved).at[taker].add(moved)
    items = jnp.searchsorted(jnp.cumsum(lengths), jnp.arange(rows * top), side="right").astype(jnp.int32)
    table = items.reshape(top, rows).T
    table = table[jax.random.permutation(jax.random.fold_in(own, 1), rows)]
    offset_by = jax.random.randint(jax.random.fold_in(own, 2), (rows, 1), 0, top)
    return jnp.take_along_axis(table, (jnp.arange(top)[None, :] + offset_by) % top, axis=1)


def load_shares(number_of, total, most, skew, full):
    weights = [(1 << 20) // math.isqrt(rank ** skew) + 1 for rank in range(1, number_of + 1)]
    largest = most if full else min(most, max(-(-total // number_of), total * weights[0] // sum(weights)))
    least = 1 if total - largest >= number_of - 1 else 0
    holding, rest = [largest] + [least] * (number_of - 1), total - largest - least * (number_of - 1)
    while rest > 0:
        candidates = [i for i in range(1, number_of) if holding[i] < largest] or [i for i in range(1, number_of) if holding[i] < most]
        pool, left = sum([weights[i] for i in candidates]), rest
        for i in candidates:
            extra = min(most - holding[i], max(1, left * weights[i] // pool), rest)
            holding[i] = holding[i] + extra
            rest = rest - extra
    return np.array(holding)


def noise(key, dims, scale, limit, pieces=(), kind=jnp.bfloat16):
    factor_of = levels(key, dims, pieces, -0.22, 0.18) if pieces else 1.0
    array = jax.random.normal(key, dims, jnp.float32) * scale * factor_of
    return jnp.minimum(jnp.maximum(array, -limit), limit).astype(kind)


def setup_inputs(seed: int = 0, part: int = 0) -> dict:
    arg_keys = jax.random.split(jax.random.key(seed), 8)
    own_keys = jax.random.split(jax.random.fold_in(arg_keys[7], part), 8)
    images = noise(own_keys[0], (BANDS, STRIPS, SUBS, BLOCK, BLOCK), 1.0, 6.0, ((0, 2), (1, 2), (2, 4)))
    mask_bits = touch_ends(jax.random.randint(own_keys[1], (BANDS, STRIPS, SUBS, BLOCK, BLOCK), 0, 8), jax.random.fold_in(own_keys[1], 1), 0, 7).astype(jnp.int32)
    inv_var = jnp.clip(jnp.exp(math.log(4.0) - 2.0794415 * jax.random.uniform(own_keys[2], (BANDS, STRIPS, SUBS), jnp.float32) ** levels(own_keys[2], (BANDS, STRIPS, SUBS), ((0, 2), (1, 2), (2, 4)), -0.2, 0.2)), 0.5, 4.0)
    routes_keys = jax.random.split(jax.random.fold_in(own_keys[3], 1), BANDS * STRIPS * SUBS // SB)
    routes_turns = jax.random.permutation(jax.random.fold_in(own_keys[3], 3), BANDS * STRIPS * SUBS // SB)
    routes = jax.vmap(lambda own, number: routed_block(jax.random.fold_in(own_keys[3], 2), own, number, SB, N_EXP, 1, CAP, 2))(routes_keys, routes_turns).reshape((BANDS, STRIPS, SUBS, 1))
    block_slot = touch_ends(jax.random.randint(own_keys[4], (BANDS, STRIPS, SUBS), 0, BLOCK_ROWS * BLOCK_COLS), jax.random.fold_in(own_keys[4], 1), 0, (BLOCK_ROWS * BLOCK_COLS) - 1).astype(jnp.int32)
    kernel_index = touch_ends(jax.random.randint(own_keys[5], (BANDS, STRIPS, SUBS), 0, NCOEF), jax.random.fold_in(own_keys[5], 1), 0, NCOEF - 1).astype(jnp.int32)
    coefficients = noise(arg_keys[6], (NCOEF, 3), 1.0, 4.0, (), jnp.float32)
    return dict(images=images, mask_bits=mask_bits, inv_var=inv_var, routes=routes, block_slot=block_slot, kernel_index=kernel_index, coefficients=coefficients)


kernel_sigmas = (1.0, 2.5, 6.0)


def usable_share(bits):
    flagged = jnp.bitwise_and(bits, 6) == 6
    suspect = jnp.bitwise_and(bits, 1).astype(jnp.float32)
    return jnp.where(flagged, 0.0, 1.0 - 0.5 * suspect).astype(jnp.float32)


def gaussian_taps(half_span):
    taps_axis = jnp.arange(-half_span, half_span + 1).astype(jnp.float32)
    result = []
    for spread in kernel_sigmas:
        values = jnp.exp(-taps_axis * taps_axis / (2.0 * spread * spread))
        result.append(values / jnp.sum(values))
    return jnp.stack(result)


def to_image(blocks):
    grid_rows, grid_cols = blocks.shape[0], blocks.shape[1]
    return blocks.transpose(0, 2, 1, 3).reshape(grid_rows * BLOCK, grid_cols * BLOCK)


def reference(images, mask_bits, inv_var, routes, block_slot, kernel_index, coefficients):
    half_span = TAPS // 2
    taps = gaussian_taps(half_span)
    grid_rows = STRIPS * BLOCK_ROWS
    grid_cols = N_EXP * BLOCK_COLS
    strip_of = jnp.repeat(jnp.arange(STRIPS, dtype=jnp.int32), SUBS)
    coadds = []
    detection = jnp.zeros((grid_rows * BLOCK, grid_cols * BLOCK), jnp.float32)
    for band_index in range(BANDS):
        usable = usable_share(mask_bits[band_index].reshape(-1, BLOCK, BLOCK))
        inverse = inv_var[band_index].reshape(-1)[:, None, None]
        weight = (usable * inverse).astype(jnp.bfloat16)
        pictures = images[band_index].reshape(-1, BLOCK, BLOCK).astype(jnp.float32)
        weighted = (usable * inverse * pictures).astype(jnp.bfloat16)
        slot_here = block_slot[band_index].reshape(-1).astype(jnp.int32)
        owner = routes[band_index].reshape(-1).astype(jnp.int32)
        block_row = (strip_of * BLOCK_ROWS + slot_here // BLOCK_COLS).astype(jnp.int32)
        block_col = (owner * BLOCK_COLS + slot_here % BLOCK_COLS).astype(jnp.int32)
        coef_rows = coefficients[kernel_index[band_index].reshape(-1).astype(jnp.int32)]
        empty = jnp.zeros((grid_rows, grid_cols, BLOCK, BLOCK), jnp.float32)
        planes = []
        for basis_index in range(3):
            contrib = coef_rows[:, basis_index][:, None, None] * weighted.astype(jnp.float32)
            planes.append(to_image(empty.at[block_row, block_col].add(contrib)))
        depth_sum = to_image(empty.at[block_row, block_col].add(weight.astype(jnp.float32)))
        stacked = jnp.stack(planes)[None]
        downward = lax.conv_general_dilated(stacked, taps[:, None, :, None], (1, 1), ((half_span, half_span), (0, 0)), dimension_numbers=("NCHW", "OIHW", "NCHW"), feature_group_count=3, precision=lax.Precision.HIGHEST)
        sideways = lax.conv_general_dilated(downward, taps[:, None, None, :], (1, 1), ((0, 0), (half_span, half_span)), dimension_numbers=("NCHW", "OIHW", "NCHW"), feature_group_count=3, precision=lax.Precision.HIGHEST)
        matched = jnp.sum(sideways[0], axis=0)
        denominator = 1.0 + depth_sum
        coadded = matched / denominator
        coadds.append(coadded)
        detection = detection + coadded * coadded * denominator
    return jnp.stack(coadds), detection
```

```python
import functools

import jax
import jax.numpy as jnp
import numpy as np
from jax import lax
from jax.experimental import pallas as pl
from jax.experimental.pallas import tpu as pltpu
from jax.sharding import PartitionSpec as P

TAPS = 41
BLOCK_ROWS = 2
BLOCK_COLS = 4
SLOTS = BLOCK_ROWS * BLOCK_COLS
SPILL = 24
CHUNKS = 4
PARTS = 4

kernel_sigmas = (1.0, 2.5, 6.0)
MESH = pl.DeviceIdType.MESH


def tap_matrix(rows, cols, shift):
    half_span = TAPS // 2
    offset = np.arange(rows)[:, None] - np.arange(cols)[None, :] - shift
    axis = np.arange(-half_span, half_span + 1).astype(np.float64)
    result = []
    for spread in kernel_sigmas:
        norm = np.sum(np.exp(-axis * axis / (2.0 * spread * spread)))
        result.append(
            np.where(
                np.abs(offset) <= half_span,
                np.exp(-offset * offset / (2.0 * spread * spread)),
                0.0,
            )
            / norm
        )
    return np.stack(result)


def tap_pair(taps):
    high = taps.astype(jnp.bfloat16)
    low = (taps - high.astype(np.float64)).astype(jnp.bfloat16)
    return jnp.asarray(np.stack([high, low]))


def split(value):
    high = value.astype(jnp.bfloat16)
    return high, (value - high.astype(jnp.float32)).astype(jnp.bfloat16)


def products(pairs):
    total = None
    for left, right in pairs:
        term = jnp.dot(left, right, preferred_element_type=jnp.float32)
        total = term if total is None else total + term
    return total


def coadd_kernel(
    n, strips, bands,
    routes, slots, kernels, inverse, coefs, images, masks, across, down,
    coadd, detection,
    pictures, bits_in, weights, raw, acc, planes, own_depth, raw_depth, table, raw_table,
    frame, result, depth_moving, moving, last_out, last_in, spilling, spilled,
    below, det_mine, det_theirs,
    in_sem, raw_send, raw_recv, table_sem, depth_send, depth_recv, send_sem, recv_sem,
    last_send, last_recv, spill_send, spill_recv, det_send, det_recv,
):
    me = lax.axis_index("exp")
    strip = lax.axis_index("tile")
    band = lax.axis_index("band")
    held, block = pictures.shape[0], pictures.shape[1]
    span = block // CHUNKS
    rows_all, tile_cols = result.shape[1:]
    part = rows_all // PARTS
    half = tile_cols // 2
    at_left, at_right = me == 0, me == n - 1
    at_end = at_left | at_right
    gets_raw_left, gets_raw_right = me == 1, me == n - 2
    left_half = 2 * me < n - 1

    def input_copies(c):
        rows = pl.ds(pl.multiple_of(c * span, span), span)
        return (
            pltpu.make_async_copy(masks.at[:, rows], bits_in.at[:, rows], in_sem.at[c, 0]),
            pltpu.make_async_copy(images.at[:, rows], pictures.at[:, rows], in_sem.at[c, 1]),
        )

    for c in range(CHUNKS):
        for copy in input_copies(c):
            copy.start()

    barrier = pltpu.get_barrier_semaphore()
    greet = [
        (strip > 0, {"tile": strip - 1}),
        (strip < strips - 1, {"tile": strip + 1}),
        (me > 0, {"exp": me - 1}),
        (me < n - 1, {"exp": me + 1}),
    ]
    peers = bands - 1
    for here, peer in greet:

        @pl.when(here)
        def _(peer=peer):
            pl.semaphore_signal(barrier, inc=1, device_id=peer, device_id_type=MESH)

        peers = peers + here.astype(jnp.int32)
    for j in range(1, bands):
        pl.semaphore_signal(
            barrier, inc=1, device_id={"band": lax.rem(band + j, bands)}, device_id_type=MESH
        )

    keys = [routes[i] * SLOTS + slots[i] for i in range(held)]
    for i in range(held):
        before = held
        for j in range(i):
            before = jnp.where(keys[j] == keys[i], j, before)
        table[i] = jnp.int32(before)

    def note_last(key, carry):
        last = held
        for i in range(held):
            last = jnp.where(routes[i] * SLOTS + slots[i] == key - SLOTS, i, last)
        table[held + key] = last
        return carry

    lax.fori_loop(0, (n + 2) * SLOTS, note_last, 0)

    def last_of(entries, d, slot):
        return entries[held + (d + 1) * SLOTS + slot]

    none = jnp.zeros((block, block), jnp.float32)
    for k in range(3):
        acc[held, k] = none
    for k in range(4):
        planes[held, k] = none.astype(jnp.bfloat16)
    own_depth[held] = none
    raw_depth[held] = none

    sends_spill = (strip < strips - 1, strip > 0)
    gets_spill = (strip > 0, strip < strips - 1)
    for side in range(2):

        @pl.when(jnp.logical_not(gets_spill[side]))
        def _(side=side):
            spilled[side] = jnp.zeros(spilled.shape[1:], spilled.dtype)

    pl.semaphore_wait(barrier, peers)

    inward = jnp.where(at_left, 1, n - 2)

    def raw_copy(c):
        return pltpu.make_async_remote_copy(
            src_ref=weights.at[c],
            dst_ref=raw.at[c],
            send_sem=raw_send.at[c],
            recv_sem=raw_recv.at[c],
            device_id={"exp": inward},
            device_id_type=MESH,
        )

    def table_copy():
        return pltpu.make_async_remote_copy(
            src_ref=table,
            dst_ref=raw_table,
            send_sem=table_sem.at[0],
            recv_sem=table_sem.at[1],
            device_id={"exp": inward},
            device_id_type=MESH,
        )

    @pl.when(at_end)
    def _():
        table_copy().start()

    def prepare(c, carry):
        for copy in input_copies(c):
            copy.wait()
        rows = pl.ds(pl.multiple_of(c * span, span), span)
        for i in range(held):
            bits = bits_in[i, rows]
            suspect = jnp.bitwise_and(bits, 1).astype(jnp.float32)
            usable = jnp.where(jnp.bitwise_and(bits, 6) == 6, 0.0, 1.0 - 0.5 * suspect)
            scaled = usable * inverse[i]
            weight = scaled.astype(jnp.bfloat16)
            weights[c, i] = weight
            weighted = (
                (scaled * pictures[i, rows].astype(jnp.float32))
                .astype(jnp.bfloat16)
                .astype(jnp.float32)
            )
            before = table[i]
            which = kernels[i]
            own_depth[i, rows] = weight.astype(jnp.float32) + own_depth[before, rows]
            sums = []
            for k in range(3):
                value = coefs[k, which] * weighted + acc[before, k, rows]
                acc[i, k, rows] = value
                sums.append(value)
            planes[i, 0, rows], planes[i, 1, rows] = split(sums[0])
            planes[i, 2, rows] = sums[1].astype(jnp.bfloat16)
            planes[i, 3, rows] = sums[2].astype(jnp.bfloat16)

        @pl.when(at_end)
        def _():
            raw_copy(c).start()

        return carry

    lax.fori_loop(0, CHUNKS, prepare, 0)

    def spill_copy(side, d):
        peer = strip + 1 if side == 0 else strip - 1
        return pltpu.make_async_remote_copy(
            src_ref=spilling.at[side, d],
            dst_ref=spilled.at[side, d],
            send_sem=spill_send.at[side, d],
            recv_sem=spill_recv.at[side, d],
            device_id={"tile": peer},
            device_id_type=MESH,
        )

    def correlate(d):
        for b in range(-1, BLOCK_COLS + 1):
            tile = d + b // BLOCK_COLS
            cols = slice((b + 1) * block, (b + 2) * block)
            for r in range(BLOCK_ROWS):
                which = last_of(table, tile, r * BLOCK_COLS + b % BLOCK_COLS)
                for k in range(4):
                    frame[k, r * block : (r + 1) * block, cols] = planes[which, k]
        first = (frame[0], frame[1])
        tall_high, tall_low = split(
            products(((down[0, 0], first[0]), (down[0, 0], first[1]), (down[1, 0], first[0])))
        )
        second = frame[2]
        tall_second = products(((down[0, 1], second), (down[1, 1], second))).astype(jnp.bfloat16)
        tall_third = products(((down[0, 2], frame[3]),)).astype(jnp.bfloat16)
        for h in range(2):
            cols = slice(h * half, h * half + half + 2 * block)
            total = products((
                (tall_high[:, cols], across[0, 0]),
                (tall_high[:, cols], across[1, 0]),
                (tall_low[:, cols], across[0, 0]),
                (tall_second[:, cols], across[0, 1]),
                (tall_second[:, cols], across[1, 1]),
                (tall_third[:, cols], across[0, 2]),
            ))
            out = slice(h * half, (h + 1) * half)
            result[d, :, out] = total[SPILL : SPILL + rows_all]
            spilling[0, d, :, out] = total[SPILL + rows_all :].astype(jnp.bfloat16)
            spilling[1, d, :, out] = total[0:SPILL].astype(jnp.bfloat16)
        for side in range(2):

            @pl.when(sends_spill[side])
            def _(side=side):
                spill_copy(side, d).start()

    def step(right, s):
        d = jnp.where(right, n - 1 - s, s)
        sends = jnp.where(right, d > me, d < me)
        gets = jnp.where(right, me > 0, me < n - 1)
        place = jnp.where(right, d, jnp.where(d == me - 1, n, d))
        return d, sends, gets, place, jnp.where(right, me + 1, me - 1)

    def arrived(ref, sems, place, c):
        pltpu.make_async_remote_copy(
            src_ref=ref.at[place, c],
            dst_ref=ref.at[place, c],
            send_sem=sems.at[place, c],
            recv_sem=sems.at[place, c],
            device_id={"band": lax.rem(band + 1, bands)},
            device_id_type=MESH,
        ).wait_recv()

    def depth_copy(right, s, c):
        d, _sends, _gets, place, target = step(right, s)
        return pltpu.make_async_remote_copy(
            src_ref=depth_moving.at[d, c],
            dst_ref=depth_moving.at[place, c],
            send_sem=depth_send.at[d, c],
            recv_sem=depth_recv.at[place, c],
            device_id={"exp": target},
            device_id_type=MESH,
        )

    def add_depth(d, c, extra):
        rows = pl.ds(pl.multiple_of(c * span, span), span)
        for r in range(BLOCK_ROWS):
            for b in range(BLOCK_COLS):
                slot = r * BLOCK_COLS + b
                cols = slice(b * block, (b + 1) * block)
                value = own_depth[last_of(table, d, slot), rows] + extra(r, slot, cols, rows)
                depth_moving[d, c, r, :, cols] = value.astype(jnp.bfloat16)

    def move_depth(right, s, c):
        d, sends, _gets, _place, _target = step(right, s)
        from_raw = jnp.where(right, gets_raw_left, gets_raw_right)

        @pl.when(sends & jnp.logical_not(at_end))
        def _():
            @pl.when(from_raw)
            def _():
                add_depth(
                    d, c,
                    lambda r, slot, cols, rows: raw_depth[last_of(raw_table, d, slot), rows],
                )

            @pl.when(jnp.logical_not(from_raw))
            def _():
                arrived(depth_moving, depth_recv, d, c)
                add_depth(
                    d, c,
                    lambda r, slot, cols, rows: depth_moving[d, c, r, :, cols].astype(jnp.float32),
                )

            depth_copy(right, s, c).start()

    def directions():
        return (left_half, jnp.logical_not(left_half))

    def depth_chunk(c):
        @pl.when(gets_raw_left | gets_raw_right)
        def _():
            @pl.when(c == 0)
            def _():
                table_copy().wait_recv()

            raw_copy(c).wait_recv()
            rows = pl.ds(pl.multiple_of(c * span, span), span)
            for i in range(held):
                raw_depth[i, rows] = raw[c, i].astype(jnp.float32) + raw_depth[raw_table[i], rows]

        def one(s, carry):
            for right in directions():
                move_depth(right, s, c)
            return carry

        lax.fori_loop(0, n - 1, one, 0)

    def complete(d):
        for side in range(2):

            @pl.when(gets_spill[side])
            def _(side=side):
                spill_copy(side, d).wait_recv()

        low = rows_all - SPILL
        result[d, 0:SPILL] += spilled[0, d].astype(jnp.float32)
        result[d, low:] += spilled[1, d].astype(jnp.float32)

    def pick(i):
        down_from = n - 1 - i
        right = jnp.where(down_from > me, down_from, down_from - 1)
        left = jnp.where(i < me, i, i + 1)
        return jnp.where(i == n - 1, me, jnp.where(left_half, right, left))

    def part_copy(right, s, q):
        d, _sends, _gets, place, target = step(right, s)
        return pltpu.make_async_remote_copy(
            src_ref=moving.at[d, q],
            dst_ref=moving.at[place, q],
            send_sem=send_sem.at[d, q],
            recv_sem=recv_sem.at[place, q],
            device_id={"exp": target},
            device_id_type=MESH,
        )

    def last_copy(q):
        target = jnp.where(me == n - 2, n - 1, 0)
        return pltpu.make_async_remote_copy(
            src_ref=last_out.at[q],
            dst_ref=last_in.at[q],
            send_sem=last_send.at[q],
            recv_sem=last_recv.at[q],
            device_id={"exp": target},
            device_id_type=MESH,
        )

    def part_rows(q):
        return pl.ds(pl.multiple_of(q * part, part), part)

    def move_first(i):
        s = i

        def one(q, carry):
            d = step(at_left, s)[0]
            moving[d, q] = result[d, part_rows(q)].astype(jnp.bfloat16)
            part_copy(at_left, s, q).start()
            return carry

        lax.fori_loop(0, PARTS, one, 0)

    def move_part(right, s, q):
        d, sends, _gets, _place, _target = step(right, s)
        to_end = jnp.where(right, me == n - 2, me == 1) & (s == 0)

        @pl.when(sends & jnp.logical_not(at_end))
        def _():
            arrived(moving, recv_sem, d, q)
            value = moving[d, q].astype(jnp.float32) + result[d, part_rows(q)]

            @pl.when(to_end)
            def _():
                last_out[q] = value
                last_copy(q).start()

            @pl.when(jnp.logical_not(to_end))
            def _():
                moving[d, q] = value.astype(jnp.bfloat16)
                part_copy(right, s, q).start()

    def turn(i, carry):
        correlate(pick(i))

        @pl.when(i > 0)
        def _():
            complete(pick(i - 1))

            @pl.when(at_end)
            def _():
                move_first(i - 1)

        @pl.when(i < CHUNKS)
        def _():
            depth_chunk(i)

        return carry

    lax.fori_loop(0, n, turn, 0)
    complete(me)
    for c in range(n, CHUNKS):
        depth_chunk(c)

    def forward(i, carry):
        for right in directions():
            move_part(right, i // PARTS, lax.rem(i, PARTS))
        return carry

    lax.fori_loop(0, (n - 1) * PARTS, forward, 0)

    def bottom(c, carry):
        chunk_rows = pl.ds(pl.multiple_of(c * span, span), span)
        for r in range(BLOCK_ROWS):
            for b in range(BLOCK_COLS):
                slot = r * BLOCK_COLS + b
                cols = slice(b * block, (b + 1) * block)
                rows = pl.ds(pl.multiple_of(r * block + c * span, span), span)
                below[rows, cols] = 1.0 + own_depth[last_of(table, me, slot), chunk_rows]

        @pl.when(gets_raw_left | gets_raw_right)
        def _():
            for r in range(BLOCK_ROWS):
                for b in range(BLOCK_COLS):
                    slot = r * BLOCK_COLS + b
                    cols = slice(b * block, (b + 1) * block)
                    rows = pl.ds(pl.multiple_of(r * block + c * span, span), span)
                    below[rows, cols] += raw_depth[last_of(raw_table, me, slot), chunk_rows]

        for has, place in (
            ((me > 1), me),
            ((me < n - 2), n),
        ):

            @pl.when(has)
            def _(place=place):
                arrived(depth_moving, depth_recv, place, c)
                for r in range(BLOCK_ROWS):
                    rows = pl.ds(pl.multiple_of(r * block + c * span, span), span)
                    below[rows] += depth_moving[place, c, r].astype(jnp.float32)

        return carry

    lax.fori_loop(0, CHUNKS, bottom, 0)

    def det_copy(j, q):
        return pltpu.make_async_remote_copy(
            src_ref=det_mine.at[part_rows(q)],
            dst_ref=det_theirs.at[j - 1, part_rows(q)],
            send_sem=det_send.at[j - 1, q],
            recv_sem=det_recv.at[j - 1, q],
            device_id={"band": lax.rem(band + j, bands)},
            device_id_type=MESH,
        )

    def finish(q, carry):
        rows = part_rows(q)

        @pl.when(at_end)
        def _():
            last_copy(q).wait_recv()
            result[me, rows] += last_in[q]

        @pl.when(jnp.logical_not(at_end))
        def _():
            arrived(moving, recv_sem, me, q)
            arrived(moving, recv_sem, n, q)
            result[me, rows] += moving[me, q].astype(jnp.float32) + moving[n, q].astype(
                jnp.float32
            )

        value = result[me, rows] / below[rows]
        coadd[rows] = value
        det_mine[rows] = value * value * below[rows]
        for j in range(1, bands):
            det_copy(j, q).start()
        return carry

    lax.fori_loop(0, PARTS, finish, 0)

    def combine(q, carry):
        rows = part_rows(q)
        value = det_mine[rows]
        for j in range(1, bands):
            det_copy(j, q).wait_recv()
            value += det_theirs[j - 1, rows]
        detection[rows] = value
        return carry

    lax.fori_loop(0, PARTS, combine, 0)

    def drain_det(q, carry):
        for j in range(1, bands):
            det_copy(j, q).wait_send()
        return carry

    lax.fori_loop(0, PARTS, drain_det, 0)

    @pl.when(at_end)
    def _():
        table_copy().wait_send()

        def drain_raw(c, carry):
            raw_copy(c).wait_send()
            return carry

        lax.fori_loop(0, CHUNKS, drain_raw, 0)

    @pl.when(jnp.logical_not(at_end))
    def _():
        def drain_depth(i, carry):
            s, c = i // CHUNKS, lax.rem(i, CHUNKS)
            for right in directions():

                @pl.when(step(right, s)[1])
                def _(right=right):
                    depth_copy(right, s, c).wait_send()

            return carry

        lax.fori_loop(0, (n - 1) * CHUNKS, drain_depth, 0)

    def drain(i, carry):
        s, q = i // PARTS, lax.rem(i, PARTS)
        for right in directions():
            to_end = jnp.where(right, me == n - 2, me == 1) & (s == 0)
            sends = step(right, s)[1]

            @pl.when(sends & to_end)
            def _():
                last_copy(q).wait_send()

            @pl.when(sends & jnp.logical_not(to_end))
            def _(right=right):
                part_copy(right, s, q).wait_send()

        return carry

    lax.fori_loop(0, (n - 1) * PARTS, drain, 0)

    def drain_spill(d, carry):
        for side in range(2):

            @pl.when(sends_spill[side])
            def _(side=side):
                spill_copy(side, d).wait_send()

        return carry

    lax.fori_loop(0, n, drain_spill, 0)


def local(sizes, images, mask_bits, inv_var, routes, block_slot, kernel_index, coefficients):
    n, strips, bands = sizes["exp"], sizes["tile"], sizes["band"]
    held, block = images.shape[2:4]
    tile_rows = BLOCK_ROWS * block
    tile_cols = BLOCK_COLS * block
    half = tile_cols // 2
    span = block // CHUNKS
    part = tile_rows // PARTS
    entries = pl.cdiv(held + (n + 2) * SLOTS, 128) * 128
    across = tap_pair(tap_matrix(2 * half, half, block))
    down = tap_pair(tap_matrix(tile_rows + 2 * SPILL, tile_rows, SPILL))
    smem = pl.BlockSpec(memory_space=pltpu.SMEM)
    vmem = pl.BlockSpec(memory_space=pltpu.VMEM)
    anywhere = pl.BlockSpec(memory_space=pl.ANY)
    whole = jax.ShapeDtypeStruct((tile_rows, tile_cols), jnp.float32)
    bf16, f32 = jnp.bfloat16, jnp.float32
    dma = pltpu.SemaphoreType.DMA
    coadd, detection = pl.pallas_call(
        functools.partial(coadd_kernel, n, strips, bands),
        out_shape=(whole, whole),
        in_specs=[smem] * 5 + [anywhere] * 2 + [vmem] * 2,
        out_specs=(vmem, vmem),
        scratch_shapes=[
            pltpu.VMEM((held, block, block), bf16),
            pltpu.VMEM((held, block, block), jnp.int32),
            pltpu.VMEM((CHUNKS, held, span, block), bf16),
            pltpu.VMEM((CHUNKS, held, span, block), bf16),
            pltpu.VMEM((held + 1, 3, block, block), f32),
            pltpu.VMEM((held + 1, 4, block, block), bf16),
            pltpu.VMEM((held + 1, block, block), f32),
            pltpu.VMEM((held + 1, block, block), f32),
            pltpu.SMEM((entries,), jnp.int32),
            pltpu.SMEM((entries,), jnp.int32),
            pltpu.VMEM((4, tile_rows, tile_cols + 2 * block), bf16),
            pltpu.VMEM((n, tile_rows, tile_cols), f32),
            pltpu.VMEM((n + 1, CHUNKS, BLOCK_ROWS, span, tile_cols), bf16),
            pltpu.VMEM((n + 1, PARTS, part, tile_cols), bf16),
            pltpu.VMEM((PARTS, part, tile_cols), f32),
            pltpu.VMEM((PARTS, part, tile_cols), f32),
            pltpu.VMEM((2, n, SPILL, tile_cols), bf16),
            pltpu.VMEM((2, n, SPILL, tile_cols), bf16),
            pltpu.VMEM((tile_rows, tile_cols), f32),
            pltpu.VMEM((tile_rows, tile_cols), f32),
            pltpu.VMEM((bands - 1, tile_rows, tile_cols), f32),
            dma((CHUNKS, 2)),
            dma((CHUNKS,)),
            dma((CHUNKS,)),
            dma((2,)),
            dma((n, CHUNKS)),
            dma((n + 1, CHUNKS)),
            dma((n, PARTS)),
            dma((n + 1, PARTS)),
            dma((PARTS,)),
            dma((PARTS,)),
            dma((2, n)),
            dma((2, n)),
            dma((bands - 1, PARTS)),
            dma((bands - 1, PARTS)),
        ],
        compiler_params=pltpu.CompilerParams(collective_id=0, has_side_effects=True),
        name="coadd",
    )(
        routes[0, 0, :, 0], block_slot[0, 0], kernel_index[0, 0], inv_var[0, 0],
        coefficients.T, images[0, 0], mask_bits[0, 0], across, down,
    )
    return coadd[None], detection


def solution(mesh):
    return jax.shard_map(
        functools.partial(local, dict(mesh.shape)),
        mesh=mesh,
        in_specs=(
            P(("patch", "band"), "tile", "exp", None, None),
            P(("patch", "band"), "tile", "exp", None, None),
            P(("patch", "band"), "tile", "exp"),
            P(("patch", "band"), "tile", "exp", None),
            P(("patch", "band"), "tile", "exp"),
            P(("patch", "band"), "tile", "exp"),
            P(),
        ),
        out_specs=(P(("patch", "band"), "tile", "exp"), P(("patch", "tile"), "exp")),
        check_vma=False,
    )
```

```python
import functools

import jax
import jax.numpy as jnp
import numpy as np
from jax import lax
from jax.experimental import pallas as pl
from jax.experimental.pallas import tpu as pltpu
from jax.sharding import PartitionSpec as P

TAPS = 41
BLOCK_ROWS = 2
BLOCK_COLS = 4
SLOTS = BLOCK_ROWS * BLOCK_COLS
SPILL = 24
CHUNKS = 4
PARTS = 4

kernel_sigmas = (1.0, 2.5, 6.0)
MESH = pl.DeviceIdType.MESH


def tap_matrix(rows, cols, shift):
    half_span = TAPS // 2
    offset = np.arange(rows)[:, None] - np.arange(cols)[None, :] - shift
    axis = np.arange(-half_span, half_span + 1).astype(np.float64)
    result = []
    for spread in kernel_sigmas:
        norm = np.sum(np.exp(-axis * axis / (2.0 * spread * spread)))
        result.append(
            np.where(
                np.abs(offset) <= half_span,
                np.exp(-offset * offset / (2.0 * spread * spread)),
                0.0,
            )
            / norm
        )
    return np.stack(result)


def tap_pair(taps):
    high = taps.astype(jnp.bfloat16)
    low = (taps - high.astype(np.float64)).astype(jnp.bfloat16)
    return jnp.asarray(np.stack([high, low]))


def split(value):
    high = value.astype(jnp.bfloat16)
    return high, (value - high.astype(jnp.float32)).astype(jnp.bfloat16)


def products(pairs):
    total = None
    for left, right in pairs:
        term = jnp.dot(left, right, preferred_element_type=jnp.float32)
        total = term if total is None else total + term
    return total


def coadd_kernel(
    n, strips, bands,
    routes, slots, kernels, inverse, coefs, images, masks, across_in, down_in,
    coadd, detection,
    across, down, pictures, bits_in, weights, raw, acc, planes, own_depth, raw_depth, table, raw_table,
    frame, result, depth_moving, moving, last_out, last_in, spilling, spilled,
    below, det_mine, det_theirs,
    taps_sem, in_sem, raw_send, raw_recv, table_sem, depth_send, depth_recv, send_sem, recv_sem,
    last_send, last_recv, spill_send, spill_recv, det_send, det_recv,
):
    me = lax.axis_index("exp")
    strip = lax.axis_index("tile")
    band = lax.axis_index("band")
    held, block = pictures.shape[0], pictures.shape[1]
    span = block // CHUNKS
    rows_all, tile_cols = result.shape[1:]
    part = rows_all // PARTS
    half = tile_cols // 2
    at_left, at_right = me == 0, me == n - 1
    at_end = at_left | at_right
    gets_raw_left, gets_raw_right = me == 1, me == n - 2
    left_half = 2 * me < n - 1

    def input_copies(c):
        rows = pl.ds(pl.multiple_of(c * span, span), span)
        return (
            pltpu.make_async_copy(masks.at[:, rows], bits_in.at[:, rows], in_sem.at[c, 0]),
            pltpu.make_async_copy(images.at[:, rows], pictures.at[:, rows], in_sem.at[c, 1]),
        )

    for c in range(CHUNKS):
        for copy in input_copies(c):
            copy.start()

    taps_copies = (
        pltpu.make_async_copy(down_in, down, taps_sem.at[0]),
        pltpu.make_async_copy(across_in, across, taps_sem.at[1]),
    )
    for copy in taps_copies:
        copy.start()

    barrier = pltpu.get_barrier_semaphore()
    greet = [
        (strip > 0, {"tile": strip - 1}),
        (strip < strips - 1, {"tile": strip + 1}),
        (me > 0, {"exp": me - 1}),
        (me < n - 1, {"exp": me + 1}),
    ]
    peers = bands - 1
    for here, peer in greet:

        @pl.when(here)
        def _(peer=peer):
            pl.semaphore_signal(barrier, inc=1, device_id=peer, device_id_type=MESH)

        peers = peers + here.astype(jnp.int32)
    for j in range(1, bands):
        pl.semaphore_signal(
            barrier, inc=1, device_id={"band": lax.rem(band + j, bands)}, device_id_type=MESH
        )

    keys = [routes[i] * SLOTS + slots[i] for i in range(held)]
    for i in range(held):
        before = held
        for j in range(i):
            before = jnp.where(keys[j] == keys[i], j, before)
        table[i] = jnp.int32(before)

    def note_last(key, carry):
        last = held
        for i in range(held):
            last = jnp.where(routes[i] * SLOTS + slots[i] == key - SLOTS, i, last)
        table[held + key] = last
        return carry

    lax.fori_loop(0, (n + 2) * SLOTS, note_last, 0)

    def last_of(entries, d, slot):
        return entries[held + (d + 1) * SLOTS + slot]

    none = jnp.zeros((block, block), jnp.float32)
    for k in range(3):
        acc[held, k] = none
    for k in range(4):
        planes[held, k] = none.astype(jnp.bfloat16)
    own_depth[held] = none
    raw_depth[held] = none

    sends_spill = (strip < strips - 1, strip > 0)
    gets_spill = (strip > 0, strip < strips - 1)
    for side in range(2):

        @pl.when(jnp.logical_not(gets_spill[side]))
        def _(side=side):
            spilled[side] = jnp.zeros(spilled.shape[1:], spilled.dtype)

    inward = jnp.where(at_left, 1, n - 2)

    def raw_copy(c):
        return pltpu.make_async_remote_copy(
            src_ref=weights.at[c],
            dst_ref=raw.at[c],
            send_sem=raw_send.at[c],
            recv_sem=raw_recv.at[c],
            device_id={"exp": inward},
            device_id_type=MESH,
        )

    def table_copy():
        return pltpu.make_async_remote_copy(
            src_ref=table,
            dst_ref=raw_table,
            send_sem=table_sem.at[0],
            recv_sem=table_sem.at[1],
            device_id={"exp": inward},
            device_id_type=MESH,
        )

    def scaled_of(i, rows):
        bits = bits_in[i, rows]
        suspect = jnp.bitwise_and(bits, 1).astype(jnp.float32)
        usable = jnp.where(jnp.bitwise_and(bits, 6) == 6, 0.0, 1.0 - 0.5 * suspect)
        return usable * inverse[i]

    def weigh(c, carry):
        input_copies(c)[0].wait()
        rows = pl.ds(pl.multiple_of(c * span, span), span)
        for i in range(held):
            weights[c, i] = scaled_of(i, rows).astype(jnp.bfloat16)
        return carry

    lax.fori_loop(0, CHUNKS, weigh, 0)
    pl.semaphore_wait(barrier, peers)

    @pl.when(at_end)
    def _():
        for c in range(CHUNKS):
            raw_copy(c).start()
        table_copy().start()

    def prepare(c, carry):
        input_copies(c)[1].wait()
        rows = pl.ds(pl.multiple_of(c * span, span), span)
        for i in range(held):
            scaled = scaled_of(i, rows)
            weighted = (
                (scaled * pictures[i, rows].astype(jnp.float32))
                .astype(jnp.bfloat16)
                .astype(jnp.float32)
            )
            before = table[i]
            which = kernels[i]
            own_depth[i, rows] = weights[c, i].astype(jnp.float32) + own_depth[before, rows]
            sums = []
            for k in range(3):
                value = coefs[k, which] * weighted + acc[before, k, rows]
                acc[i, k, rows] = value
                sums.append(value)
            planes[i, 0, rows], planes[i, 1, rows] = split(sums[0])
            planes[i, 2, rows] = sums[1].astype(jnp.bfloat16)
            planes[i, 3, rows] = sums[2].astype(jnp.bfloat16)

        return carry

    lax.fori_loop(0, CHUNKS, prepare, 0)

    for copy in taps_copies:
        copy.wait()

    def spill_copy(side, d):
        peer = strip + 1 if side == 0 else strip - 1
        return pltpu.make_async_remote_copy(
            src_ref=spilling.at[side, d],
            dst_ref=spilled.at[side, d],
            send_sem=spill_send.at[side, d],
            recv_sem=spill_recv.at[side, d],
            device_id={"tile": peer},
            device_id_type=MESH,
        )

    def correlate(d):
        for b in range(-1, BLOCK_COLS + 1):
            tile = d + b // BLOCK_COLS
            cols = slice((b + 1) * block, (b + 2) * block)
            for r in range(BLOCK_ROWS):
                which = last_of(table, tile, r * BLOCK_COLS + b % BLOCK_COLS)
                for k in range(4):
                    frame[k, r * block : (r + 1) * block, cols] = planes[which, k]
        first = (frame[0], frame[1])
        tall_high, tall_low = split(
            products(((down[0, 0], first[0]), (down[0, 0], first[1]), (down[1, 0], first[0])))
        )
        second = frame[2]
        tall_second = products(((down[0, 1], second), (down[1, 1], second))).astype(jnp.bfloat16)
        tall_third = products(((down[0, 2], frame[3]),)).astype(jnp.bfloat16)
        for h in range(2):
            cols = slice(h * half, h * half + half + 2 * block)
            total = products((
                (tall_high[:, cols], across[0, 0]),
                (tall_high[:, cols], across[1, 0]),
                (tall_low[:, cols], across[0, 0]),
                (tall_second[:, cols], across[0, 1]),
                (tall_second[:, cols], across[1, 1]),
                (tall_third[:, cols], across[0, 2]),
            ))
            out = slice(h * half, (h + 1) * half)
            result[d, :, out] = total[SPILL : SPILL + rows_all]
            spilling[0, d, :, out] = total[SPILL + rows_all :].astype(jnp.bfloat16)
            spilling[1, d, :, out] = total[0:SPILL].astype(jnp.bfloat16)
        for side in range(2):

            @pl.when(sends_spill[side])
            def _(side=side):
                spill_copy(side, d).start()

    def step(right, s):
        d = jnp.where(right, n - 1 - s, s)
        sends = jnp.where(right, d > me, d < me)
        gets = jnp.where(right, me > 0, me < n - 1)
        place = jnp.where(right, d, jnp.where(d == me - 1, n, d))
        return d, sends, gets, place, jnp.where(right, me + 1, me - 1)

    def arrived(ref, sems, place, c):
        pltpu.make_async_remote_copy(
            src_ref=ref.at[place, c],
            dst_ref=ref.at[place, c],
            send_sem=sems.at[place, c],
            recv_sem=sems.at[place, c],
            device_id={"band": lax.rem(band + 1, bands)},
            device_id_type=MESH,
        ).wait_recv()

    def depth_copy(right, s, c):
        d, _sends, _gets, place, target = step(right, s)
        return pltpu.make_async_remote_copy(
            src_ref=depth_moving.at[d, c],
            dst_ref=depth_moving.at[place, c],
            send_sem=depth_send.at[d, c],
            recv_sem=depth_recv.at[place, c],
            device_id={"exp": target},
            device_id_type=MESH,
        )

    def add_depth(d, c, extra):
        rows = pl.ds(pl.multiple_of(c * span, span), span)
        for r in range(BLOCK_ROWS):
            for b in range(BLOCK_COLS):
                slot = r * BLOCK_COLS + b
                cols = slice(b * block, (b + 1) * block)
                value = own_depth[last_of(table, d, slot), rows] + extra(r, slot, cols, rows)
                depth_moving[d, c, r, :, cols] = value.astype(jnp.bfloat16)

    def move_depth(right, s, c):
        d, sends, _gets, _place, _target = step(right, s)
        from_raw = jnp.where(right, gets_raw_left, gets_raw_right)

        @pl.when(sends & jnp.logical_not(at_end))
        def _():
            @pl.when(from_raw)
            def _():
                add_depth(
                    d, c,
                    lambda r, slot, cols, rows: raw_depth[last_of(raw_table, d, slot), rows],
                )

            @pl.when(jnp.logical_not(from_raw))
            def _():
                arrived(depth_moving, depth_recv, d, c)
                add_depth(
                    d, c,
                    lambda r, slot, cols, rows: depth_moving[d, c, r, :, cols].astype(jnp.float32),
                )

            depth_copy(right, s, c).start()

    def directions():
        return (left_half, jnp.logical_not(left_half))

    def lag(right):
        return jnp.where(right, me - 1, n - 2 - me)

    def depth_slot(t):
        @pl.when((gets_raw_left | gets_raw_right) & (t < CHUNKS))
        def _():
            @pl.when(t == 0)
            def _():
                table_copy().wait_recv()

            raw_copy(t).wait_recv()
            rows = pl.ds(pl.multiple_of(t * span, span), span)
            for i in range(held):
                raw_depth[i, rows] = raw[t, i].astype(jnp.float32) + raw_depth[raw_table[i], rows]

        def one(s, carry):
            for right in directions():
                c = t - lag(right)

                @pl.when((c >= 0) & (c < CHUNKS))
                def _(right=right, c=c):
                    move_depth(right, s, c)

            return carry

        lax.fori_loop(0, n - 1, one, 0)

    def complete(d):
        for side in range(2):

            @pl.when(gets_spill[side])
            def _(side=side):
                spill_copy(side, d).wait_recv()

        low = rows_all - SPILL
        result[d, 0:SPILL] += spilled[0, d].astype(jnp.float32)
        result[d, low:] += spilled[1, d].astype(jnp.float32)

    def pick(i):
        down_from = n - 1 - i
        right = jnp.where(down_from > me, down_from, down_from - 1)
        left = jnp.where(i < me, i, i + 1)
        return jnp.where(i == n - 1, me, jnp.where(left_half, right, left))

    def part_copy(right, s, q):
        d, _sends, _gets, place, target = step(right, s)
        return pltpu.make_async_remote_copy(
            src_ref=moving.at[d, q],
            dst_ref=moving.at[place, q],
            send_sem=send_sem.at[d, q],
            recv_sem=recv_sem.at[place, q],
            device_id={"exp": target},
            device_id_type=MESH,
        )

    def last_copy(q):
        target = jnp.where(me == n - 2, n - 1, 0)
        return pltpu.make_async_remote_copy(
            src_ref=last_out.at[q],
            dst_ref=last_in.at[q],
            send_sem=last_send.at[q],
            recv_sem=last_recv.at[q],
            device_id={"exp": target},
            device_id_type=MESH,
        )

    def part_rows(q):
        return pl.ds(pl.multiple_of(q * part, part), part)

    def move_first(i):
        s = i

        def one(q, carry):
            d = step(at_left, s)[0]
            moving[d, q] = result[d, part_rows(q)].astype(jnp.bfloat16)
            part_copy(at_left, s, q).start()
            return carry

        lax.fori_loop(0, PARTS, one, 0)

    def move_part(right, s, q):
        d, sends, _gets, _place, _target = step(right, s)
        to_end = jnp.where(right, me == n - 2, me == 1) & (s == 0)

        @pl.when(sends & jnp.logical_not(at_end))
        def _():
            arrived(moving, recv_sem, d, q)
            value = moving[d, q].astype(jnp.float32) + result[d, part_rows(q)]

            @pl.when(to_end)
            def _():
                last_out[q] = value
                last_copy(q).start()

            @pl.when(jnp.logical_not(to_end))
            def _():
                moving[d, q] = value.astype(jnp.bfloat16)
                part_copy(right, s, q).start()

    def turn(i, carry):
        correlate(pick(i))

        @pl.when(i > 0)
        def _():
            complete(pick(i - 1))

            @pl.when(at_end)
            def _():
                move_first(i - 1)

        depth_slot(i)
        return carry

    lax.fori_loop(0, n, turn, 0)
    complete(me)
    for t in range(n, CHUNKS + n - 3):
        depth_slot(t)

    def forward(t, carry):
        for right in directions():
            i = t - lag(right)

            @pl.when((i >= 0) & (i < (n - 1) * PARTS))
            def _(right=right, i=i):
                move_part(right, i // PARTS, lax.rem(i, PARTS))

        return carry

    lax.fori_loop(0, (n - 1) * PARTS + n - 3, forward, 0)

    def bottom(c, carry):
        chunk_rows = pl.ds(pl.multiple_of(c * span, span), span)
        for r in range(BLOCK_ROWS):
            for b in range(BLOCK_COLS):
                slot = r * BLOCK_COLS + b
                cols = slice(b * block, (b + 1) * block)
                rows = pl.ds(pl.multiple_of(r * block + c * span, span), span)
                below[rows, cols] = 1.0 + own_depth[last_of(table, me, slot), chunk_rows]

        @pl.when(gets_raw_left | gets_raw_right)
        def _():
            for r in range(BLOCK_ROWS):
                for b in range(BLOCK_COLS):
                    slot = r * BLOCK_COLS + b
                    cols = slice(b * block, (b + 1) * block)
                    rows = pl.ds(pl.multiple_of(r * block + c * span, span), span)
                    below[rows, cols] += raw_depth[last_of(raw_table, me, slot), chunk_rows]

        for has, place in (
            ((me > 1), me),
            ((me < n - 2), n),
        ):

            @pl.when(has)
            def _(place=place):
                arrived(depth_moving, depth_recv, place, c)
                for r in range(BLOCK_ROWS):
                    rows = pl.ds(pl.multiple_of(r * block + c * span, span), span)
                    below[rows] += depth_moving[place, c, r].astype(jnp.float32)

        return carry

    lax.fori_loop(0, CHUNKS, bottom, 0)

    def det_copy(j, q):
        return pltpu.make_async_remote_copy(
            src_ref=det_mine.at[part_rows(q)],
            dst_ref=det_theirs.at[j - 1, part_rows(q)],
            send_sem=det_send.at[j - 1, q],
            recv_sem=det_recv.at[j - 1, q],
            device_id={"band": lax.rem(band + j, bands)},
            device_id_type=MESH,
        )

    def finish(q, carry):
        rows = part_rows(q)

        @pl.when(at_end)
        def _():
            last_copy(q).wait_recv()
            result[me, rows] += last_in[q]

        @pl.when(jnp.logical_not(at_end))
        def _():
            arrived(moving, recv_sem, me, q)
            arrived(moving, recv_sem, n, q)
            result[me, rows] += moving[me, q].astype(jnp.float32) + moving[n, q].astype(
                jnp.float32
            )

        value = result[me, rows] / below[rows]
        coadd[rows] = value
        det_mine[rows] = value * value * below[rows]
        for j in range(1, bands):
            det_copy(j, q).start()
        return carry

    lax.fori_loop(0, PARTS, finish, 0)

    def combine(q, carry):
        rows = part_rows(q)
        value = det_mine[rows]
        for j in range(1, bands):
            det_copy(j, q).wait_recv()
            value += det_theirs[j - 1, rows]
        detection[rows] = value
        return carry

    lax.fori_loop(0, PARTS, combine, 0)

    def drain_det(q, carry):
        for j in range(1, bands):
            det_copy(j, q).wait_send()
        return carry

    lax.fori_loop(0, PARTS, drain_det, 0)

    @pl.when(at_end)
    def _():
        table_copy().wait_send()

        def drain_raw(c, carry):
            raw_copy(c).wait_send()
            return carry

        lax.fori_loop(0, CHUNKS, drain_raw, 0)

    @pl.when(jnp.logical_not(at_end))
    def _():
        def drain_depth(i, carry):
            s, c = i // CHUNKS, lax.rem(i, CHUNKS)
            for right in directions():

                @pl.when(step(right, s)[1])
                def _(right=right):
                    depth_copy(right, s, c).wait_send()

            return carry

        lax.fori_loop(0, (n - 1) * CHUNKS, drain_depth, 0)

    def drain(i, carry):
        s, q = i // PARTS, lax.rem(i, PARTS)
        for right in directions():
            to_end = jnp.where(right, me == n - 2, me == 1) & (s == 0)
            sends = step(right, s)[1]

            @pl.when(sends & to_end)
            def _():
                last_copy(q).wait_send()

            @pl.when(sends & jnp.logical_not(to_end))
            def _(right=right):
                part_copy(right, s, q).wait_send()

        return carry

    lax.fori_loop(0, (n - 1) * PARTS, drain, 0)

    def drain_spill(d, carry):
        for side in range(2):

            @pl.when(sends_spill[side])
            def _(side=side):
                spill_copy(side, d).wait_send()

        return carry

    lax.fori_loop(0, n, drain_spill, 0)


def local(sizes, images, mask_bits, inv_var, routes, block_slot, kernel_index, coefficients):
    n, strips, bands = sizes["exp"], sizes["tile"], sizes["band"]
    held, block = images.shape[2:4]
    tile_rows = BLOCK_ROWS * block
    tile_cols = BLOCK_COLS * block
    half = tile_cols // 2
    span = block // CHUNKS
    part = tile_rows // PARTS
    entries = pl.cdiv(held + (n + 2) * SLOTS, 128) * 128
    across = tap_pair(tap_matrix(2 * half, half, block))
    down = tap_pair(tap_matrix(tile_rows + 2 * SPILL, tile_rows, SPILL))
    smem = pl.BlockSpec(memory_space=pltpu.SMEM)
    vmem = pl.BlockSpec(memory_space=pltpu.VMEM)
    anywhere = pl.BlockSpec(memory_space=pltpu.HBM)
    whole = jax.ShapeDtypeStruct((tile_rows, tile_cols), jnp.float32)
    bf16, f32 = jnp.bfloat16, jnp.float32
    dma = pltpu.SemaphoreType.DMA
    scratch = [
        pltpu.VMEM(across.shape, bf16),
        pltpu.VMEM(down.shape, bf16),
        pltpu.VMEM((held, block, block), bf16),
        pltpu.VMEM((held, block, block), jnp.int32),
        pltpu.VMEM((CHUNKS, held, span, block), bf16),
        pltpu.VMEM((CHUNKS, held, span, block), bf16),
        pltpu.VMEM((held + 1, 3, block, block), f32),
        pltpu.VMEM((held + 1, 4, block, block), bf16),
        pltpu.VMEM((held + 1, block, block), f32),
        pltpu.VMEM((held + 1, block, block), f32),
        pltpu.SMEM((entries,), jnp.int32),
        pltpu.SMEM((entries,), jnp.int32),
        pltpu.VMEM((4, tile_rows, tile_cols + 2 * block), bf16),
        pltpu.VMEM((n, tile_rows, tile_cols), f32),
        pltpu.VMEM((n + 1, CHUNKS, BLOCK_ROWS, span, tile_cols), bf16),
        pltpu.VMEM((n + 1, PARTS, part, tile_cols), bf16),
        pltpu.VMEM((PARTS, part, tile_cols), f32),
        pltpu.VMEM((PARTS, part, tile_cols), f32),
        pltpu.VMEM((2, n, SPILL, tile_cols), bf16),
        pltpu.VMEM((2, n, SPILL, tile_cols), bf16),
        pltpu.VMEM((tile_rows, tile_cols), f32),
        pltpu.VMEM((tile_rows, tile_cols), f32),
        pltpu.VMEM((bands - 1, tile_rows, tile_cols), f32),
        dma((2,)),
        dma((CHUNKS, 2)),
        dma((CHUNKS,)),
        dma((CHUNKS,)),
        dma((2,)),
        dma((n, CHUNKS)),
        dma((n + 1, CHUNKS)),
        dma((n, PARTS)),
        dma((n + 1, PARTS)),
        dma((PARTS,)),
        dma((PARTS,)),
        dma((2, n)),
        dma((2, n)),
        dma((bands - 1, PARTS)),
        dma((bands - 1, PARTS)),
    ]
    held_bytes = sum(
        int(np.prod(x.shape)) * jnp.dtype(x.dtype).itemsize
        for x in scratch
        if x.memory_space == pltpu.VMEM
    )
    limit = min(held_bytes + (16 << 20), 60 * 1024 * 1024)
    coadd, detection = pl.pallas_call(
        functools.partial(coadd_kernel, n, strips, bands),
        out_shape=(whole, whole),
        in_specs=[smem] * 5 + [anywhere] * 4,
        out_specs=(vmem, vmem),
        scratch_shapes=scratch,
        compiler_params=pltpu.CompilerParams(collective_id=0, has_side_effects=True, vmem_limit_bytes=limit),
        name="coadd",
    )(*[
        pltpu.with_memory_space_constraint(x, pltpu.HBM)
        for x in (
            routes[0, 0, :, 0], block_slot[0, 0], kernel_index[0, 0], inv_var[0, 0],
            coefficients.T, images[0, 0], mask_bits[0, 0], across, down,
        )
    ])
    return coadd[None], detection


def solution(mesh):
    return jax.shard_map(
        functools.partial(local, dict(mesh.shape)),
        mesh=mesh,
        in_specs=(
            P(("patch", "band"), "tile", "exp", None, None),
            P(("patch", "band"), "tile", "exp", None, None),
            P(("patch", "band"), "tile", "exp"),
            P(("patch", "band"), "tile", "exp", None),
            P(("patch", "band"), "tile", "exp"),
            P(("patch", "band"), "tile", "exp"),
            P(),
        ),
        out_specs=(P(("patch", "band"), "tile", "exp"), P(("patch", "tile"), "exp")),
        check_vma=False,
    )
```

```python
import functools

import jax
import jax.numpy as jnp
import numpy as np
from jax import lax
from jax.experimental import pallas as pl
from jax.experimental.pallas import tpu as pltpu
from jax.sharding import PartitionSpec as P

TAPS = 41
BLOCK_ROWS = 2
BLOCK_COLS = 4
SLOTS = BLOCK_ROWS * BLOCK_COLS
SPILL = 24
CHUNKS = 4
PARTS = 8
LAG = 2

kernel_sigmas = (1.0, 2.5, 6.0)
MESH = pl.DeviceIdType.MESH


def tap_matrix(rows, cols, shift):
    half_span = TAPS // 2
    offset = np.arange(rows)[:, None] - np.arange(cols)[None, :] - shift
    axis = np.arange(-half_span, half_span + 1).astype(np.float64)
    result = []
    for spread in kernel_sigmas:
        norm = np.sum(np.exp(-axis * axis / (2.0 * spread * spread)))
        result.append(
            np.where(
                np.abs(offset) <= half_span,
                np.exp(-offset * offset / (2.0 * spread * spread)),
                0.0,
            )
            / norm
        )
    return np.stack(result)


def tap_pair(taps):
    high = taps.astype(jnp.bfloat16)
    low = (taps - high.astype(np.float64)).astype(jnp.bfloat16)
    return jnp.asarray(np.stack([high, low]))


def split(value):
    high = value.astype(jnp.bfloat16)
    return high, (value - high.astype(jnp.float32)).astype(jnp.bfloat16)


def products(pairs):
    total = None
    for left, right in pairs:
        term = jnp.dot(left, right, preferred_element_type=jnp.float32)
        total = term if total is None else total + term
    return total


def coadd_kernel(
    n, strips, bands,
    routes, slots, kernels, inverse, coefs, images, masks, across_in, down_in,
    coadd, detection,
    across, down, pictures, bits_in, weights, raw, acc, planes, own_depth, raw_depth, table, raw_table,
    frame, result, depth_moving, moving, last_out, last_in, spilling, spilled,
    below, det_mine, det_theirs,
    taps_sem, in_sem, raw_send, raw_recv, table_sem, depth_send, depth_recv, send_sem, recv_sem,
    last_send, last_recv, spill_send, spill_recv, det_send, det_recv,
):
    me = lax.axis_index("exp")
    strip = lax.axis_index("tile")
    band = lax.axis_index("band")
    held, block = pictures.shape[0], pictures.shape[1]
    span = block // CHUNKS
    rows_all, tile_cols = result.shape[1:]
    part = rows_all // PARTS
    half = tile_cols // 2
    at_left, at_right = me == 0, me == n - 1
    at_end = at_left | at_right
    gets_raw_left, gets_raw_right = me == 1, me == n - 2
    left_half = 2 * me < n - 1

    def input_copies(c):
        rows = pl.ds(pl.multiple_of(c * span, span), span)
        return (
            pltpu.make_async_copy(masks.at[:, rows], bits_in.at[:, rows], in_sem.at[c, 0]),
            pltpu.make_async_copy(images.at[:, rows], pictures.at[:, rows], in_sem.at[c, 1]),
        )

    for c in range(CHUNKS):
        for copy in input_copies(c):
            copy.start()

    taps_copies = (
        pltpu.make_async_copy(down_in, down, taps_sem.at[0]),
        pltpu.make_async_copy(across_in, across, taps_sem.at[1]),
    )
    for copy in taps_copies:
        copy.start()

    barrier = pltpu.get_barrier_semaphore()
    greet = [
        (strip > 0, {"tile": strip - 1}),
        (strip < strips - 1, {"tile": strip + 1}),
        (me > 0, {"exp": me - 1}),
        (me < n - 1, {"exp": me + 1}),
    ]
    peers = bands - 1
    for here, peer in greet:

        @pl.when(here)
        def _(peer=peer):
            pl.semaphore_signal(barrier, inc=1, device_id=peer, device_id_type=MESH)

        peers = peers + here.astype(jnp.int32)
    for j in range(1, bands):
        pl.semaphore_signal(
            barrier, inc=1, device_id={"band": lax.rem(band + j, bands)}, device_id_type=MESH
        )

    def last_of(entries, d, slot):
        return entries[held + (d + 1) * SLOTS + slot]

    inward = jnp.where(at_left, 1, n - 2)

    def raw_copy(c):
        return pltpu.make_async_remote_copy(
            src_ref=weights.at[c],
            dst_ref=raw.at[c],
            send_sem=raw_send.at[c],
            recv_sem=raw_recv.at[c],
            device_id={"exp": inward},
            device_id_type=MESH,
        )

    def table_copy():
        return pltpu.make_async_remote_copy(
            src_ref=table,
            dst_ref=raw_table,
            send_sem=table_sem.at[0],
            recv_sem=table_sem.at[1],
            device_id={"exp": inward},
            device_id_type=MESH,
        )

    def scaled_of(i, rows):
        bits = bits_in[i, rows]
        suspect = jnp.bitwise_and(bits, 1).astype(jnp.float32)
        usable = jnp.where(jnp.bitwise_and(bits, 6) == 6, 0.0, 1.0 - 0.5 * suspect)
        return usable * inverse[i]

    def weigh(c, carry):
        input_copies(c)[0].wait()
        rows = pl.ds(pl.multiple_of(c * span, span), span)
        for i in range(held):
            weights[c, i] = scaled_of(i, rows).astype(jnp.bfloat16)
        return carry

    weigh(0, 0)
    pl.semaphore_wait(barrier, peers)

    @pl.when(at_end)
    def _():
        raw_copy(0).start()

    keys = [routes[i] * SLOTS + slots[i] for i in range(held)]
    for i in range(held):
        before = held
        for j in range(i):
            before = jnp.where(keys[j] == keys[i], j, before)
        table[i] = jnp.int32(before)

    def note_last(key, carry):
        last = held
        for i in range(held):
            last = jnp.where(routes[i] * SLOTS + slots[i] == key - SLOTS, i, last)
        table[held + key] = last
        return carry

    lax.fori_loop(0, (n + 2) * SLOTS, note_last, 0)

    @pl.when(at_end)
    def _():
        table_copy().start()

    def weigh_and_send(c, carry):
        weigh(c, 0)

        @pl.when(at_end)
        def _():
            raw_copy(c).start()

        return carry

    lax.fori_loop(1, CHUNKS, weigh_and_send, 0)

    none = jnp.zeros((block, block), jnp.float32)
    for k in range(3):
        acc[held, k] = none
    for k in range(4):
        planes[held, k] = none.astype(jnp.bfloat16)
    own_depth[held] = none
    raw_depth[held] = none

    sends_spill = (strip < strips - 1, strip > 0)
    gets_spill = (strip > 0, strip < strips - 1)
    for side in range(2):

        @pl.when(jnp.logical_not(gets_spill[side]))
        def _(side=side):
            spilled[side] = jnp.zeros(spilled.shape[1:], spilled.dtype)


    def prepare(c, carry):
        input_copies(c)[1].wait()
        rows = pl.ds(pl.multiple_of(c * span, span), span)
        for i in range(held):
            scaled = scaled_of(i, rows)
            weighted = (
                (scaled * pictures[i, rows].astype(jnp.float32))
                .astype(jnp.bfloat16)
                .astype(jnp.float32)
            )
            before = table[i]
            which = kernels[i]
            own_depth[i, rows] = weights[c, i].astype(jnp.float32) + own_depth[before, rows]
            sums = []
            for k in range(3):
                value = coefs[k, which] * weighted + acc[before, k, rows]
                acc[i, k, rows] = value
                sums.append(value)
            planes[i, 0, rows], planes[i, 1, rows] = split(sums[0])
            planes[i, 2, rows] = sums[1].astype(jnp.bfloat16)
            planes[i, 3, rows] = sums[2].astype(jnp.bfloat16)

        return carry

    lax.fori_loop(0, CHUNKS, prepare, 0)

    for copy in taps_copies:
        copy.wait()

    def spill_copy(side, d):
        peer = strip + 1 if side == 0 else strip - 1
        return pltpu.make_async_remote_copy(
            src_ref=spilling.at[side, d],
            dst_ref=spilled.at[side, d],
            send_sem=spill_send.at[side, d],
            recv_sem=spill_recv.at[side, d],
            device_id={"tile": peer},
            device_id_type=MESH,
        )

    def correlate(d):
        for b in range(-1, BLOCK_COLS + 1):
            tile = d + b // BLOCK_COLS
            cols = slice((b + 1) * block, (b + 2) * block)
            for r in range(BLOCK_ROWS):
                which = last_of(table, tile, r * BLOCK_COLS + b % BLOCK_COLS)
                for k in range(4):
                    frame[k, r * block : (r + 1) * block, cols] = planes[which, k]
        first = (frame[0], frame[1])
        tall_high, tall_low = split(
            products(((down[0, 0], first[0]), (down[0, 0], first[1]), (down[1, 0], first[0])))
        )
        second = frame[2]
        tall_second = products(((down[0, 1], second), (down[1, 1], second))).astype(jnp.bfloat16)
        tall_third = products(((down[0, 2], frame[3]),)).astype(jnp.bfloat16)
        for h in range(2):
            cols = slice(h * half, h * half + half + 2 * block)
            total = products((
                (tall_high[:, cols], across[0, 0]),
                (tall_high[:, cols], across[1, 0]),
                (tall_low[:, cols], across[0, 0]),
                (tall_second[:, cols], across[0, 1]),
                (tall_second[:, cols], across[1, 1]),
                (tall_third[:, cols], across[0, 2]),
            ))
            out = slice(h * half, (h + 1) * half)
            result[d, :, out] = total[SPILL : SPILL + rows_all]
            spilling[0, d, :, out] = total[SPILL + rows_all :].astype(jnp.bfloat16)
            spilling[1, d, :, out] = total[0:SPILL].astype(jnp.bfloat16)
        for side in range(2):

            @pl.when(sends_spill[side])
            def _(side=side):
                spill_copy(side, d).start()

    def step(right, s):
        d = jnp.where(right, n - 1 - s, s)
        sends = jnp.where(right, d > me, d < me)
        gets = jnp.where(right, me > 0, me < n - 1)
        place = jnp.where(right, d, jnp.where(d == me - 1, n, d))
        return d, sends, gets, place, jnp.where(right, me + 1, me - 1)

    def arrived(ref, sems, place, c):
        pltpu.make_async_remote_copy(
            src_ref=ref.at[place, c],
            dst_ref=ref.at[place, c],
            send_sem=sems.at[place, c],
            recv_sem=sems.at[place, c],
            device_id={"band": lax.rem(band + 1, bands)},
            device_id_type=MESH,
        ).wait_recv()

    def depth_copy(right, s, c):
        d, _sends, _gets, place, target = step(right, s)
        return pltpu.make_async_remote_copy(
            src_ref=depth_moving.at[d, c],
            dst_ref=depth_moving.at[place, c],
            send_sem=depth_send.at[d, c],
            recv_sem=depth_recv.at[place, c],
            device_id={"exp": target},
            device_id_type=MESH,
        )

    def add_depth(d, c, extra):
        rows = pl.ds(pl.multiple_of(c * span, span), span)
        for r in range(BLOCK_ROWS):
            for b in range(BLOCK_COLS):
                slot = r * BLOCK_COLS + b
                cols = slice(b * block, (b + 1) * block)
                value = own_depth[last_of(table, d, slot), rows] + extra(r, slot, cols, rows)
                depth_moving[d, c, r, :, cols] = value.astype(jnp.bfloat16)

    def move_depth(right, s, c):
        d, sends, _gets, _place, _target = step(right, s)
        from_raw = jnp.where(right, gets_raw_left, gets_raw_right)

        @pl.when(sends & jnp.logical_not(at_end))
        def _():
            @pl.when(from_raw)
            def _():
                add_depth(
                    d, c,
                    lambda r, slot, cols, rows: raw_depth[last_of(raw_table, d, slot), rows],
                )

            @pl.when(jnp.logical_not(from_raw))
            def _():
                arrived(depth_moving, depth_recv, d, c)
                add_depth(
                    d, c,
                    lambda r, slot, cols, rows: depth_moving[d, c, r, :, cols].astype(jnp.float32),
                )

            depth_copy(right, s, c).start()

    def directions():
        return (left_half, jnp.logical_not(left_half))

    def lag(right):
        return LAG * jnp.where(right, me - 1, n - 2 - me)

    def depth_slot(t):
        @pl.when((gets_raw_left | gets_raw_right) & (t < CHUNKS))
        def _():
            @pl.when(t == 0)
            def _():
                table_copy().wait_recv()

            raw_copy(t).wait_recv()
            rows = pl.ds(pl.multiple_of(t * span, span), span)
            for i in range(held):
                raw_depth[i, rows] = raw[t, i].astype(jnp.float32) + raw_depth[raw_table[i], rows]

        def one(s, carry):
            for right in directions():
                c = t - lag(right)

                @pl.when((c >= 0) & (c < CHUNKS))
                def _(right=right, c=c):
                    move_depth(right, s, c)

            return carry

        lax.fori_loop(0, n - 1, one, 0)

    def complete(d):
        for side in range(2):

            @pl.when(gets_spill[side])
            def _(side=side):
                spill_copy(side, d).wait_recv()

        low = rows_all - SPILL
        result[d, 0:SPILL] += spilled[0, d].astype(jnp.float32)
        result[d, low:] += spilled[1, d].astype(jnp.float32)

    def pick(i):
        down_from = n - 1 - i
        right = jnp.where(down_from > me, down_from, down_from - 1)
        left = jnp.where(i < me, i, i + 1)
        return jnp.where(i == n - 1, me, jnp.where(left_half, right, left))

    def part_copy(right, s, q):
        d, _sends, _gets, place, target = step(right, s)
        return pltpu.make_async_remote_copy(
            src_ref=moving.at[d, q],
            dst_ref=moving.at[place, q],
            send_sem=send_sem.at[d, q],
            recv_sem=recv_sem.at[place, q],
            device_id={"exp": target},
            device_id_type=MESH,
        )

    def last_copy(q):
        target = jnp.where(me == n - 2, n - 1, 0)
        return pltpu.make_async_remote_copy(
            src_ref=last_out.at[q],
            dst_ref=last_in.at[q],
            send_sem=last_send.at[q],
            recv_sem=last_recv.at[q],
            device_id={"exp": target},
            device_id_type=MESH,
        )

    def part_rows(q):
        return pl.ds(pl.multiple_of(q * part, part), part)

    def move_first(i):
        s = i

        def one(q, carry):
            d = step(at_left, s)[0]
            moving[d, q] = result[d, part_rows(q)].astype(jnp.bfloat16)
            part_copy(at_left, s, q).start()
            return carry

        lax.fori_loop(0, PARTS, one, 0)

    def move_part(right, s, q):
        d, sends, _gets, _place, _target = step(right, s)
        to_end = jnp.where(right, me == n - 2, me == 1) & (s == 0)

        @pl.when(sends & jnp.logical_not(at_end))
        def _():
            arrived(moving, recv_sem, d, q)
            value = moving[d, q].astype(jnp.float32) + result[d, part_rows(q)]

            @pl.when(to_end)
            def _():
                last_out[q] = value
                last_copy(q).start()

            @pl.when(jnp.logical_not(to_end))
            def _():
                moving[d, q] = value.astype(jnp.bfloat16)
                part_copy(right, s, q).start()

    per_turn = pl.cdiv(CHUNKS, n)

    def turn(i, carry):
        correlate(pick(i))

        @pl.when(i > 0)
        def _():
            complete(pick(i - 1))

            @pl.when(at_end)
            def _():
                move_first(i - 1)

        for k in range(per_turn):
            depth_slot(i * per_turn + k)
        return carry

    lax.fori_loop(0, n, turn, 0)
    complete(me)

    def late_slot(t, carry):
        depth_slot(t)
        return carry

    lax.fori_loop(n * per_turn, CHUNKS + LAG * (n - 3), late_slot, 0)

    def forward(t, carry):
        for right in directions():
            i = t - lag(right)

            @pl.when((i >= 0) & (i < (n - 1) * PARTS))
            def _(right=right, i=i):
                move_part(right, i // PARTS, lax.rem(i, PARTS))

        return carry

    lax.fori_loop(0, (n - 1) * PARTS + LAG * (n - 3), forward, 0)

    def bottom(c, carry):
        chunk_rows = pl.ds(pl.multiple_of(c * span, span), span)
        for r in range(BLOCK_ROWS):
            for b in range(BLOCK_COLS):
                slot = r * BLOCK_COLS + b
                cols = slice(b * block, (b + 1) * block)
                rows = pl.ds(pl.multiple_of(r * block + c * span, span), span)
                below[rows, cols] = 1.0 + own_depth[last_of(table, me, slot), chunk_rows]

        @pl.when(gets_raw_left | gets_raw_right)
        def _():
            for r in range(BLOCK_ROWS):
                for b in range(BLOCK_COLS):
                    slot = r * BLOCK_COLS + b
                    cols = slice(b * block, (b + 1) * block)
                    rows = pl.ds(pl.multiple_of(r * block + c * span, span), span)
                    below[rows, cols] += raw_depth[last_of(raw_table, me, slot), chunk_rows]

        for has, place in (
            ((me > 1), me),
            ((me < n - 2), n),
        ):

            @pl.when(has)
            def _(place=place):
                arrived(depth_moving, depth_recv, place, c)
                for r in range(BLOCK_ROWS):
                    rows = pl.ds(pl.multiple_of(r * block + c * span, span), span)
                    below[rows] += depth_moving[place, c, r].astype(jnp.float32)

        return carry

    lax.fori_loop(0, CHUNKS, bottom, 0)

    def det_copy(j, q):
        return pltpu.make_async_remote_copy(
            src_ref=det_mine.at[part_rows(q)],
            dst_ref=det_theirs.at[j - 1, part_rows(q)],
            send_sem=det_send.at[j - 1, q],
            recv_sem=det_recv.at[j - 1, q],
            device_id={"band": lax.rem(band + j, bands)},
            device_id_type=MESH,
        )

    def finish(q, carry):
        rows = part_rows(q)

        @pl.when(at_end)
        def _():
            last_copy(q).wait_recv()
            result[me, rows] += last_in[q]

        @pl.when(jnp.logical_not(at_end))
        def _():
            arrived(moving, recv_sem, me, q)
            arrived(moving, recv_sem, n, q)
            result[me, rows] += moving[me, q].astype(jnp.float32) + moving[n, q].astype(
                jnp.float32
            )

        value = result[me, rows] / below[rows]
        coadd[rows] = value
        det_mine[rows] = value * value * below[rows]
        for j in range(1, bands):
            det_copy(j, q).start()
        return carry

    lax.fori_loop(0, PARTS, finish, 0)

    @pl.when(at_end)
    def _():
        table_copy().wait_send()

        def drain_raw(c, carry):
            raw_copy(c).wait_send()
            return carry

        lax.fori_loop(0, CHUNKS, drain_raw, 0)

    @pl.when(jnp.logical_not(at_end))
    def _():
        def drain_depth(i, carry):
            s, c = i // CHUNKS, lax.rem(i, CHUNKS)
            for right in directions():

                @pl.when(step(right, s)[1])
                def _(right=right):
                    depth_copy(right, s, c).wait_send()

            return carry

        lax.fori_loop(0, (n - 1) * CHUNKS, drain_depth, 0)

    def drain(i, carry):
        s, q = i // PARTS, lax.rem(i, PARTS)
        for right in directions():
            to_end = jnp.where(right, me == n - 2, me == 1) & (s == 0)
            sends = step(right, s)[1]

            @pl.when(sends & to_end)
            def _():
                last_copy(q).wait_send()

            @pl.when(sends & jnp.logical_not(to_end))
            def _(right=right):
                part_copy(right, s, q).wait_send()

        return carry

    lax.fori_loop(0, (n - 1) * PARTS, drain, 0)

    def drain_spill(d, carry):
        for side in range(2):

            @pl.when(sends_spill[side])
            def _(side=side):
                spill_copy(side, d).wait_send()

        return carry

    lax.fori_loop(0, n, drain_spill, 0)

    def combine(q, carry):
        rows = part_rows(q)
        value = det_mine[rows]
        for j in range(1, bands):
            det_copy(j, q).wait_recv()
            value += det_theirs[j - 1, rows]
        detection[rows] = value
        return carry

    lax.fori_loop(0, PARTS, combine, 0)

    def drain_det(q, carry):
        for j in range(1, bands):
            det_copy(j, q).wait_send()
        return carry

    lax.fori_loop(0, PARTS, drain_det, 0)


def local(sizes, images, mask_bits, inv_var, routes, block_slot, kernel_index, coefficients):
    n, strips, bands = sizes["exp"], sizes["tile"], sizes["band"]
    held, block = images.shape[2:4]
    tile_rows = BLOCK_ROWS * block
    tile_cols = BLOCK_COLS * block
    half = tile_cols // 2
    span = block // CHUNKS
    part = tile_rows // PARTS
    entries = pl.cdiv(held + (n + 2) * SLOTS, 128) * 128
    across = tap_pair(tap_matrix(2 * half, half, block))
    down = tap_pair(tap_matrix(tile_rows + 2 * SPILL, tile_rows, SPILL))
    smem = pl.BlockSpec(memory_space=pltpu.SMEM)
    vmem = pl.BlockSpec(memory_space=pltpu.VMEM)
    anywhere = pl.BlockSpec(memory_space=pltpu.HBM)
    whole = jax.ShapeDtypeStruct((tile_rows, tile_cols), jnp.float32)
    bf16, f32 = jnp.bfloat16, jnp.float32
    dma = pltpu.SemaphoreType.DMA
    scratch = [
        pltpu.VMEM(across.shape, bf16),
        pltpu.VMEM(down.shape, bf16),
        pltpu.VMEM((held, block, block), bf16),
        pltpu.VMEM((held, block, block), jnp.int32),
        pltpu.VMEM((CHUNKS, held, span, block), bf16),
        pltpu.VMEM((CHUNKS, held, span, block), bf16),
        pltpu.VMEM((held + 1, 3, block, block), f32),
        pltpu.VMEM((held + 1, 4, block, block), bf16),
        pltpu.VMEM((held + 1, block, block), f32),
        pltpu.VMEM((held + 1, block, block), f32),
        pltpu.SMEM((entries,), jnp.int32),
        pltpu.SMEM((entries,), jnp.int32),
        pltpu.VMEM((4, tile_rows, tile_cols + 2 * block), bf16),
        pltpu.VMEM((n, tile_rows, tile_cols), f32),
        pltpu.VMEM((n + 1, CHUNKS, BLOCK_ROWS, span, tile_cols), bf16),
        pltpu.VMEM((n + 1, PARTS, part, tile_cols), bf16),
        pltpu.VMEM((PARTS, part, tile_cols), f32),
        pltpu.VMEM((PARTS, part, tile_cols), f32),
        pltpu.VMEM((2, n, SPILL, tile_cols), bf16),
        pltpu.VMEM((2, n, SPILL, tile_cols), bf16),
        pltpu.VMEM((tile_rows, tile_cols), f32),
        pltpu.VMEM((tile_rows, tile_cols), f32),
        pltpu.VMEM((bands - 1, tile_rows, tile_cols), f32),
        dma((2,)),
        dma((CHUNKS, 2)),
        dma((CHUNKS,)),
        dma((CHUNKS,)),
        dma((2,)),
        dma((n, CHUNKS)),
        dma((n + 1, CHUNKS)),
        dma((n, PARTS)),
        dma((n + 1, PARTS)),
        dma((PARTS,)),
        dma((PARTS,)),
        dma((2, n)),
        dma((2, n)),
        dma((bands - 1, PARTS)),
        dma((bands - 1, PARTS)),
    ]
    held_bytes = sum(
        int(np.prod(x.shape)) * jnp.dtype(x.dtype).itemsize
        for x in scratch
        if x.memory_space == pltpu.VMEM
    )
    limit = min(held_bytes + (16 << 20), 60 * 1024 * 1024)
    coadd, detection = pl.pallas_call(
        functools.partial(coadd_kernel, n, strips, bands),
        out_shape=(whole, whole),
        in_specs=[smem] * 5 + [anywhere] * 4,
        out_specs=(vmem, vmem),
        scratch_shapes=scratch,
        compiler_params=pltpu.CompilerParams(collective_id=0, has_side_effects=True, vmem_limit_bytes=limit),
        name="coadd",
    )(*[
        pltpu.with_memory_space_constraint(x, pltpu.HBM)
        for x in (
            routes[0, 0, :, 0], block_slot[0, 0], kernel_index[0, 0], inv_var[0, 0],
            coefficients.T, images[0, 0], mask_bits[0, 0], across, down,
        )
    ])
    return coadd[None], detection


def solution(mesh):
    return jax.shard_map(
        functools.partial(local, dict(mesh.shape)),
        mesh=mesh,
        in_specs=(
            P(("patch", "band"), "tile", "exp", None, None),
            P(("patch", "band"), "tile", "exp", None, None),
            P(("patch", "band"), "tile", "exp"),
            P(("patch", "band"), "tile", "exp", None),
            P(("patch", "band"), "tile", "exp"),
            P(("patch", "band"), "tile", "exp"),
            P(),
        ),
        out_specs=(P(("patch", "band"), "tile", "exp"), P(("patch", "tile"), "exp")),
        check_vma=False,
    )
```

```python
import functools

import jax
import jax.numpy as jnp
import numpy as np
from jax import lax
from jax.experimental import pallas as pl
from jax.experimental.pallas import tpu as pltpu
from jax.sharding import PartitionSpec as P

TAPS = 41
BLOCK_ROWS = 2
BLOCK_COLS = 4
SLOTS = BLOCK_ROWS * BLOCK_COLS
SPILL = 24
CHUNKS = 4
PARTS = 8
STRIDE = 4
EARLY = 3
LAG = 6

kernel_sigmas = (1.0, 2.5, 6.0)
MESH = pl.DeviceIdType.MESH


def tap_matrix(rows, cols, shift):
    half_span = TAPS // 2
    offset = np.arange(rows)[:, None] - np.arange(cols)[None, :] - shift
    axis = np.arange(-half_span, half_span + 1).astype(np.float64)
    result = []
    for spread in kernel_sigmas:
        norm = np.sum(np.exp(-axis * axis / (2.0 * spread * spread)))
        result.append(
            np.where(
                np.abs(offset) <= half_span,
                np.exp(-offset * offset / (2.0 * spread * spread)),
                0.0,
            )
            / norm
        )
    return np.stack(result)


def tap_pair(taps):
    high = taps.astype(jnp.bfloat16)
    low = (taps - high.astype(np.float64)).astype(jnp.bfloat16)
    return jnp.asarray(np.stack([high, low]))


def split(value):
    high = value.astype(jnp.bfloat16)
    return high, (value - high.astype(jnp.float32)).astype(jnp.bfloat16)


def products(pairs):
    total = None
    for left, right in pairs:
        term = jnp.dot(left, right, preferred_element_type=jnp.float32)
        total = term if total is None else total + term
    return total


def coadd_kernel(
    n, strips, bands,
    routes, slots, kernels, inverse, coefs, images, masks, across_in, down_in,
    coadd_out, detection_out,
    coadd, detection, across, down, pictures, bits_in, weights, raw, acc, planes, own_depth, raw_depth, table, raw_table,
    frame, result, depth_moving, moving, last_out, last_in, spilling, spilled,
    below, det_mine, det_theirs,
    taps_sem, in_sem, raw_send, raw_recv, table_sem, depth_send, depth_recv, send_sem, recv_sem,
    last_send, last_recv, spill_send, spill_recv, det_send, det_recv, out_sem,
):
    me = lax.axis_index("exp")
    strip = lax.axis_index("tile")
    band = lax.axis_index("band")
    held, block = pictures.shape[0], pictures.shape[1]
    span = block // CHUNKS
    rows_all, tile_cols = result.shape[1:]
    part = rows_all // PARTS
    half = tile_cols // 2
    at_left, at_right = me == 0, me == n - 1
    at_end = at_left | at_right
    gets_raw_left, gets_raw_right = me == 1, me == n - 2
    left_half = 2 * me < n - 1

    def input_copies(c):
        rows = pl.ds(pl.multiple_of(c * span, span), span)
        return (
            pltpu.make_async_copy(masks.at[:, rows], bits_in.at[:, rows], in_sem.at[c, 0]),
            pltpu.make_async_copy(images.at[:, rows], pictures.at[:, rows], in_sem.at[c, 1]),
        )

    for c in range(CHUNKS):
        for copy in input_copies(c):
            copy.start()

    taps_copies = (
        pltpu.make_async_copy(down_in, down, taps_sem.at[0]),
        pltpu.make_async_copy(across_in, across, taps_sem.at[1]),
    )
    for copy in taps_copies:
        copy.start()

    barrier = pltpu.get_barrier_semaphore()
    greet = [
        (strip > 0, {"tile": strip - 1}),
        (strip < strips - 1, {"tile": strip + 1}),
        (me > 0, {"exp": me - 1}),
        (me < n - 1, {"exp": me + 1}),
    ]
    peers = bands - 1
    for here, peer in greet:

        @pl.when(here)
        def _(peer=peer):
            pl.semaphore_signal(barrier, inc=1, device_id=peer, device_id_type=MESH)

        peers = peers + here.astype(jnp.int32)
    for j in range(1, bands):
        pl.semaphore_signal(
            barrier, inc=1, device_id={"band": lax.rem(band + j, bands)}, device_id_type=MESH
        )

    def last_of(entries, d, slot):
        return entries[held + (d + 1) * SLOTS + slot]

    inward = jnp.where(at_left, 1, n - 2)

    def raw_copy(c):
        return pltpu.make_async_remote_copy(
            src_ref=weights.at[c],
            dst_ref=raw.at[c],
            send_sem=raw_send.at[0],
            recv_sem=raw_recv.at[c],
            device_id={"exp": inward},
            device_id_type=MESH,
        )

    def table_copy():
        return pltpu.make_async_remote_copy(
            src_ref=table,
            dst_ref=raw_table,
            send_sem=table_sem.at[0],
            recv_sem=table_sem.at[1],
            device_id={"exp": inward},
            device_id_type=MESH,
        )

    def scaled_of(i, rows):
        bits = bits_in[i, rows]
        suspect = jnp.bitwise_and(bits, 1).astype(jnp.float32)
        usable = jnp.where(jnp.bitwise_and(bits, 6) == 6, 0.0, 1.0 - 0.5 * suspect)
        return usable * inverse[i]

    def weigh(c, carry):
        input_copies(c)[0].wait()
        rows = pl.ds(pl.multiple_of(c * span, span), span)
        for i in range(held):
            weights[c, i] = scaled_of(i, rows).astype(jnp.bfloat16)
        return carry

    weigh(0, 0)
    pl.semaphore_wait(barrier, peers)

    @pl.when(at_end)
    def _():
        raw_copy(0).start()

    keys = [routes[i] * SLOTS + slots[i] for i in range(held)]
    for i in range(held):
        before = held
        for j in range(i):
            before = jnp.where(keys[j] == keys[i], j, before)
        table[i] = jnp.int32(before)

    def note_last(key, carry):
        last = held
        for i in range(held):
            last = jnp.where(routes[i] * SLOTS + slots[i] == key - SLOTS, i, last)
        table[held + key] = last
        return carry

    lax.fori_loop(0, (n + 2) * SLOTS, note_last, 0)

    @pl.when(at_end)
    def _():
        table_copy().start()

    def weigh_and_send(c, carry):
        weigh(c, 0)

        @pl.when(at_end)
        def _():
            raw_copy(c).start()

        return carry

    lax.fori_loop(1, EARLY, weigh_and_send, 0)
    for c in range(EARLY, CHUNKS):
        weigh(c, 0)

    none = jnp.zeros((block, block), jnp.float32)
    for k in range(3):
        acc[held, k] = none
    for k in range(4):
        planes[held, k] = none.astype(jnp.bfloat16)
    own_depth[held] = none
    raw_depth[held] = none

    sends_spill = (strip < strips - 1, strip > 0)
    gets_spill = (strip > 0, strip < strips - 1)
    for side in range(2):

        @pl.when(jnp.logical_not(gets_spill[side]))
        def _(side=side):
            spilled[side] = jnp.zeros(spilled.shape[1:], spilled.dtype)


    def prepare(c, carry):
        input_copies(c)[1].wait()
        rows = pl.ds(pl.multiple_of(c * span, span), span)
        for i in range(held):
            scaled = scaled_of(i, rows)
            weighted = (
                (scaled * pictures[i, rows].astype(jnp.float32))
                .astype(jnp.bfloat16)
                .astype(jnp.float32)
            )
            before = table[i]
            which = kernels[i]
            own_depth[i, rows] = weights[c, i].astype(jnp.float32) + own_depth[before, rows]
            sums = []
            for k in range(3):
                value = coefs[k, which] * weighted + acc[before, k, rows]
                acc[i, k, rows] = value
                sums.append(value)
            planes[i, 0, rows], planes[i, 1, rows] = split(sums[0])
            planes[i, 2, rows] = sums[1].astype(jnp.bfloat16)
            planes[i, 3, rows] = sums[2].astype(jnp.bfloat16)

        return carry

    lax.fori_loop(0, CHUNKS, prepare, 0)

    for copy in taps_copies:
        copy.wait()

    def spill_copy(side, d):
        peer = strip + 1 if side == 0 else strip - 1
        return pltpu.make_async_remote_copy(
            src_ref=spilling.at[side, d],
            dst_ref=spilled.at[side, d],
            send_sem=spill_send.at[side],
            recv_sem=spill_recv.at[side, d],
            device_id={"tile": peer},
            device_id_type=MESH,
        )

    def correlate(d):
        for b in range(-1, BLOCK_COLS + 1):
            tile = d + b // BLOCK_COLS
            cols = slice((b + 1) * block, (b + 2) * block)
            for r in range(BLOCK_ROWS):
                which = last_of(table, tile, r * BLOCK_COLS + b % BLOCK_COLS)
                for k in range(4):
                    frame[k, r * block : (r + 1) * block, cols] = planes[which, k]
        first = (frame[0], frame[1])
        tall_high, tall_low = split(
            products(((down[0, 0], first[0]), (down[0, 0], first[1]), (down[1, 0], first[0])))
        )
        second = frame[2]
        tall_second = products(((down[0, 1], second), (down[1, 1], second))).astype(jnp.bfloat16)
        tall_third = products(((down[0, 2], frame[3]),)).astype(jnp.bfloat16)
        for h in range(2):
            cols = slice(h * half, h * half + half + 2 * block)
            total = products((
                (tall_high[:, cols], across[0, 0]),
                (tall_high[:, cols], across[1, 0]),
                (tall_low[:, cols], across[0, 0]),
                (tall_second[:, cols], across[0, 1]),
                (tall_second[:, cols], across[1, 1]),
                (tall_third[:, cols], across[0, 2]),
            ))
            out = slice(h * half, (h + 1) * half)
            result[d, :, out] = total[SPILL : SPILL + rows_all]
            spilling[0, d, :, out] = total[SPILL + rows_all :].astype(jnp.bfloat16)
            spilling[1, d, :, out] = total[0:SPILL].astype(jnp.bfloat16)
        for side in range(2):

            @pl.when(sends_spill[side])
            def _(side=side):
                spill_copy(side, d).start()

    def step(right, s):
        d = jnp.where(right, n - 1 - s, s)
        sends = jnp.where(right, d > me, d < me)
        gets = jnp.where(right, me > 0, me < n - 1)
        place = jnp.where(right, d, jnp.where(d == me - 1, n, d))
        return d, sends, gets, place, jnp.where(right, me + 1, me - 1)

    def arrived(ref, sems, place, c):
        pltpu.make_async_remote_copy(
            src_ref=ref.at[place, c],
            dst_ref=ref.at[place, c],
            send_sem=sems.at[place, c],
            recv_sem=sems.at[place, c],
            device_id={"band": lax.rem(band + 1, bands)},
            device_id_type=MESH,
        ).wait_recv()

    def depth_copy(right, s, c):
        d, _sends, _gets, place, target = step(right, s)
        return pltpu.make_async_remote_copy(
            src_ref=depth_moving.at[d, c],
            dst_ref=depth_moving.at[place, c],
            send_sem=depth_send.at[d],
            recv_sem=depth_recv.at[place, c],
            device_id={"exp": target},
            device_id_type=MESH,
        )

    def add_depth(d, c, extra):
        rows = pl.ds(pl.multiple_of(c * span, span), span)
        for r in range(BLOCK_ROWS):
            for b in range(BLOCK_COLS):
                slot = r * BLOCK_COLS + b
                cols = slice(b * block, (b + 1) * block)
                value = own_depth[last_of(table, d, slot), rows] + extra(r, slot, cols, rows)
                depth_moving[d, c, r, :, cols] = value.astype(jnp.bfloat16)

    def move_depth(right, s, c):
        d, sends, _gets, _place, _target = step(right, s)
        from_raw = jnp.where(right, gets_raw_left, gets_raw_right)

        @pl.when(sends & jnp.logical_not(at_end))
        def _():
            @pl.when(from_raw)
            def _():
                add_depth(
                    d, c,
                    lambda r, slot, cols, rows: raw_depth[last_of(raw_table, d, slot), rows],
                )

            @pl.when(jnp.logical_not(from_raw))
            def _():
                arrived(depth_moving, depth_recv, d, c)
                add_depth(
                    d, c,
                    lambda r, slot, cols, rows: depth_moving[d, c, r, :, cols].astype(jnp.float32),
                )

            depth_copy(right, s, c).start()

    def directions():
        return (left_half, jnp.logical_not(left_half))

    def lag(right):
        return LAG * jnp.where(right, me - 1, n - 2 - me)

    def take_raw(c):
        @pl.when(c == 0)
        def _():
            table_copy().wait_recv()

        raw_copy(c).wait_recv()
        rows = pl.ds(pl.multiple_of(c * span, span), span)
        for i in range(held):
            raw_depth[i, rows] = raw[c, i].astype(jnp.float32) + raw_depth[raw_table[i], rows]

    def complete(d):
        for side in range(2):

            @pl.when(gets_spill[side])
            def _(side=side):
                spill_copy(side, d).wait_recv()

        low = rows_all - SPILL
        result[d, 0:SPILL] += spilled[0, d].astype(jnp.float32)
        result[d, low:] += spilled[1, d].astype(jnp.float32)

    def pick(i):
        down_from = n - 1 - i
        right = jnp.where(down_from > me, down_from, down_from - 1)
        left = jnp.where(i < me, i, i + 1)
        return jnp.where(i == n - 1, me, jnp.where(left_half, right, left))

    def part_copy(right, s, q):
        d, _sends, _gets, place, target = step(right, s)
        return pltpu.make_async_remote_copy(
            src_ref=moving.at[d, q],
            dst_ref=moving.at[place, q],
            send_sem=send_sem.at[d],
            recv_sem=recv_sem.at[place, q],
            device_id={"exp": target},
            device_id_type=MESH,
        )

    def last_copy(q):
        target = jnp.where(me == n - 2, n - 1, 0)
        return pltpu.make_async_remote_copy(
            src_ref=last_out.at[q],
            dst_ref=last_in.at[q],
            send_sem=last_send.at[0],
            recv_sem=last_recv.at[q],
            device_id={"exp": target},
            device_id_type=MESH,
        )

    def part_rows(q):
        return pl.ds(pl.multiple_of(q * part, part), part)

    def move_first(i):
        s = i

        def one(q, carry):
            d = step(at_left, s)[0]
            moving[d, q] = result[d, part_rows(q)].astype(jnp.bfloat16)
            part_copy(at_left, s, q).start()
            return carry

        lax.fori_loop(0, PARTS, one, 0)

    def move_part(right, s, q):
        d, sends, _gets, _place, _target = step(right, s)
        to_end = jnp.where(right, me == n - 2, me == 1) & (s == 0)

        @pl.when(sends & jnp.logical_not(at_end))
        def _():
            arrived(moving, recv_sem, d, q)
            value = moving[d, q].astype(jnp.float32) + result[d, part_rows(q)]

            @pl.when(to_end)
            def _():
                last_out[q] = value
                last_copy(q).start()

            @pl.when(jnp.logical_not(to_end))
            def _():
                moving[d, q] = value.astype(jnp.bfloat16)
                part_copy(right, s, q).start()

    early, late = EARLY * STRIDE, (CHUNKS - EARLY) * STRIDE
    events = early + late + (n - 1) * PARTS

    def slot(t, carry):
        for right in directions():
            e = t - lag(right)
            in_early = e < early
            in_late = (e >= early + PARTS) & (e < early + PARTS + late)
            of_depth = jnp.where(in_early, e, e - PARTS)
            is_depth = (e >= 0) & (in_early | in_late)

            @pl.when(is_depth & (lax.rem(of_depth, STRIDE) == 0))
            def _(right=right, of_depth=of_depth):
                c = of_depth // STRIDE

                @pl.when(jnp.where(right, gets_raw_left, gets_raw_right))
                def _():
                    take_raw(c)

                def one(s, carry):
                    move_depth(right, s, c)
                    return carry

                lax.fori_loop(0, n - 1, one, 0)

            @pl.when((e >= early) & (e < events) & jnp.logical_not(is_depth))
            def _(right=right, e=e):
                i = jnp.where(e < early + PARTS, e - early, e - early - late)
                move_part(right, i // PARTS, lax.rem(i, PARTS))

        return carry

    def turn(i, carry):
        correlate(pick(i))

        @pl.when(i > 0)
        def _():
            complete(pick(i - 1))

            @pl.when(at_end)
            def _():
                move_first(i - 1)

                @pl.when(i == 1)
                def _():
                    for c in range(EARLY, CHUNKS):
                        raw_copy(c).start()

        @pl.when((i < EARLY) & jnp.logical_not(at_end))
        def _():
            lax.fori_loop(i * STRIDE, (i + 1) * STRIDE, slot, 0)

        return carry

    lax.fori_loop(0, n, turn, 0)

    @pl.when(jnp.logical_not(at_end))
    def _():
        lax.fori_loop(early, events + LAG * (n - 3), slot, 0)

    complete(me)

    def bottom(c, carry):
        chunk_rows = pl.ds(pl.multiple_of(c * span, span), span)
        for r in range(BLOCK_ROWS):
            for b in range(BLOCK_COLS):
                slot = r * BLOCK_COLS + b
                cols = slice(b * block, (b + 1) * block)
                rows = pl.ds(pl.multiple_of(r * block + c * span, span), span)
                below[rows, cols] = 1.0 + own_depth[last_of(table, me, slot), chunk_rows]

        @pl.when(gets_raw_left | gets_raw_right)
        def _():
            for r in range(BLOCK_ROWS):
                for b in range(BLOCK_COLS):
                    slot = r * BLOCK_COLS + b
                    cols = slice(b * block, (b + 1) * block)
                    rows = pl.ds(pl.multiple_of(r * block + c * span, span), span)
                    below[rows, cols] += raw_depth[last_of(raw_table, me, slot), chunk_rows]

        for has, place in (
            ((me > 1), me),
            ((me < n - 2), n),
        ):

            @pl.when(has)
            def _(place=place):
                arrived(depth_moving, depth_recv, place, c)
                for r in range(BLOCK_ROWS):
                    rows = pl.ds(pl.multiple_of(r * block + c * span, span), span)
                    below[rows] += depth_moving[place, c, r].astype(jnp.float32)

        return carry

    lax.fori_loop(0, CHUNKS, bottom, 0)

    def det_copy(j, q):
        return pltpu.make_async_remote_copy(
            src_ref=det_mine.at[part_rows(q)],
            dst_ref=det_theirs.at[j - 1, part_rows(q)],
            send_sem=det_send.at[j - 1],
            recv_sem=det_recv.at[j - 1, q],
            device_id={"band": lax.rem(band + j, bands)},
            device_id_type=MESH,
        )

    def out_copy(k, q):
        rows = part_rows(q)
        if k == 0:
            return pltpu.make_async_copy(coadd.at[rows], coadd_out.at[rows], out_sem.at[k])
        return pltpu.make_async_copy(detection.at[rows], detection_out.at[rows], out_sem.at[k])

    def finish(q, carry):
        rows = part_rows(q)

        @pl.when(at_end)
        def _():
            last_copy(q).wait_recv()
            result[me, rows] += last_in[q]

        @pl.when(jnp.logical_not(at_end))
        def _():
            arrived(moving, recv_sem, me, q)
            arrived(moving, recv_sem, n, q)
            result[me, rows] += moving[me, q].astype(jnp.float32) + moving[n, q].astype(
                jnp.float32
            )

        value = result[me, rows] / below[rows]
        coadd[rows] = value
        out_copy(0, q).start()
        det_mine[rows] = value * value * below[rows]
        for j in range(1, bands):
            det_copy(j, q).start()
        return carry

    lax.fori_loop(0, PARTS, finish, 0)

    def sent(ref, sem):
        pltpu.make_async_remote_copy(
            src_ref=ref,
            dst_ref=ref,
            send_sem=sem,
            recv_sem=sem,
            device_id={"band": lax.rem(band + 1, bands)},
            device_id_type=MESH,
        ).wait_send()

    @pl.when(at_end)
    def _():
        table_copy().wait_send()
        sent(weights, raw_send.at[0])

    def drain(s, carry):
        for right in directions():
            d, sends, _gets, _place, _target = step(right, s)
            to_end = jnp.where(right, me == n - 2, me == 1) & (s == 0)

            @pl.when(sends & jnp.logical_not(at_end))
            def _(d=d):
                sent(depth_moving.at[d], depth_send.at[d])

            @pl.when(sends & to_end)
            def _():
                sent(last_out, last_send.at[0])

            @pl.when(sends & jnp.logical_not(to_end))
            def _(d=d):
                sent(moving.at[d], send_sem.at[d])

        return carry

    lax.fori_loop(0, n - 1, drain, 0)

    for side in range(2):

        @pl.when(sends_spill[side])
        def _(side=side):
            sent(spilling.at[side], spill_send.at[side])

    def combine(q, carry):
        rows = part_rows(q)
        value = det_mine[rows]
        for j in range(1, bands):
            det_copy(j, q).wait_recv()
            value += det_theirs[j - 1, rows]
        detection[rows] = value
        out_copy(1, q).start()
        return carry

    lax.fori_loop(0, PARTS, combine, 0)

    for j in range(1, bands):
        sent(det_mine, det_send.at[j - 1])
    pltpu.make_async_copy(coadd, coadd_out, out_sem.at[0]).wait()
    pltpu.make_async_copy(detection, detection_out, out_sem.at[1]).wait()


def local(sizes, images, mask_bits, inv_var, routes, block_slot, kernel_index, coefficients):
    n, strips, bands = sizes["exp"], sizes["tile"], sizes["band"]
    held, block = images.shape[2:4]
    tile_rows = BLOCK_ROWS * block
    tile_cols = BLOCK_COLS * block
    half = tile_cols // 2
    span = block // CHUNKS
    part = tile_rows // PARTS
    entries = pl.cdiv(held + (n + 2) * SLOTS, 128) * 128
    across = tap_pair(tap_matrix(2 * half, half, block))
    down = tap_pair(tap_matrix(tile_rows + 2 * SPILL, tile_rows, SPILL))
    smem = pl.BlockSpec(memory_space=pltpu.SMEM)
    vmem = pl.BlockSpec(memory_space=pltpu.VMEM)
    anywhere = pl.BlockSpec(memory_space=pltpu.HBM)
    whole = jax.ShapeDtypeStruct((tile_rows, tile_cols), jnp.float32)
    bf16, f32 = jnp.bfloat16, jnp.float32
    dma = pltpu.SemaphoreType.DMA
    scratch = [
        pltpu.VMEM((tile_rows, tile_cols), f32),
        pltpu.VMEM((tile_rows, tile_cols), f32),
        pltpu.VMEM(across.shape, bf16),
        pltpu.VMEM(down.shape, bf16),
        pltpu.VMEM((held, block, block), bf16),
        pltpu.VMEM((held, block, block), jnp.int32),
        pltpu.VMEM((CHUNKS, held, span, block), bf16),
        pltpu.VMEM((CHUNKS, held, span, block), bf16),
        pltpu.VMEM((held + 1, 3, block, block), f32),
        pltpu.VMEM((held + 1, 4, block, block), bf16),
        pltpu.VMEM((held + 1, block, block), f32),
        pltpu.VMEM((held + 1, block, block), f32),
        pltpu.SMEM((entries,), jnp.int32),
        pltpu.SMEM((entries,), jnp.int32),
        pltpu.VMEM((4, tile_rows, tile_cols + 2 * block), bf16),
        pltpu.VMEM((n, tile_rows, tile_cols), f32),
        pltpu.VMEM((n + 1, CHUNKS, BLOCK_ROWS, span, tile_cols), bf16),
        pltpu.VMEM((n + 1, PARTS, part, tile_cols), bf16),
        pltpu.VMEM((PARTS, part, tile_cols), f32),
        pltpu.VMEM((PARTS, part, tile_cols), f32),
        pltpu.VMEM((2, n, SPILL, tile_cols), bf16),
        pltpu.VMEM((2, n, SPILL, tile_cols), bf16),
        pltpu.VMEM((tile_rows, tile_cols), f32),
        pltpu.VMEM((tile_rows, tile_cols), f32),
        pltpu.VMEM((bands - 1, tile_rows, tile_cols), f32),
        dma((2,)),
        dma((CHUNKS, 2)),
        dma((1,)),
        dma((CHUNKS,)),
        dma((2,)),
        dma((n,)),
        dma((n + 1, CHUNKS)),
        dma((n,)),
        dma((n + 1, PARTS)),
        dma((1,)),
        dma((PARTS,)),
        dma((2,)),
        dma((2, n)),
        dma((bands - 1,)),
        dma((bands - 1, PARTS)),
        dma((2,)),
    ]
    held_bytes = sum(
        int(np.prod(x.shape)) * jnp.dtype(x.dtype).itemsize
        for x in scratch
        if x.memory_space == pltpu.VMEM
    )
    limit = min(held_bytes + (16 << 20), 60 * 1024 * 1024)
    coadd, detection = pl.pallas_call(
        functools.partial(coadd_kernel, n, strips, bands),
        out_shape=(whole, whole),
        in_specs=[smem] * 5 + [anywhere] * 4,
        out_specs=(pl.BlockSpec(memory_space=pl.ANY),) * 2,
        scratch_shapes=scratch,
        compiler_params=pltpu.CompilerParams(collective_id=0, has_side_effects=True, vmem_limit_bytes=limit),
        name="coadd",
    )(*[
        pltpu.with_memory_space_constraint(x, pltpu.HBM)
        for x in (
            routes[0, 0, :, 0], block_slot[0, 0], kernel_index[0, 0], inv_var[0, 0],
            coefficients.T, images[0, 0], mask_bits[0, 0], across, down,
        )
    ])
    return coadd[None], detection


def solution(mesh):
    return jax.shard_map(
        functools.partial(local, dict(mesh.shape)),
        mesh=mesh,
        in_specs=(
            P(("patch", "band"), "tile", "exp", None, None),
            P(("patch", "band"), "tile", "exp", None, None),
            P(("patch", "band"), "tile", "exp"),
            P(("patch", "band"), "tile", "exp", None),
            P(("patch", "band"), "tile", "exp"),
            P(("patch", "band"), "tile", "exp"),
            P(),
        ),
        out_specs=(P(("patch", "band"), "tile", "exp"), P(("patch", "tile"), "exp")),
        check_vma=False,
    )
```

```python
import functools

import jax
import jax.numpy as jnp
import numpy as np
from jax import lax
from jax.experimental import pallas as pl
from jax.experimental.pallas import tpu as pltpu
from jax.sharding import PartitionSpec as P

TAPS = 41
BLOCK_ROWS = 2
BLOCK_COLS = 4
SLOTS = BLOCK_ROWS * BLOCK_COLS
SPILL = 24
CHUNKS = 4
PARTS = 8
STRIDE = 4
EARLY = 3
WIDE = 4
LAG = 6

kernel_sigmas = (1.0, 2.5, 6.0)
MESH = pl.DeviceIdType.MESH


def tap_matrix(rows, cols, shift):
    half_span = TAPS // 2
    offset = np.arange(rows)[:, None] - np.arange(cols)[None, :] - shift
    axis = np.arange(-half_span, half_span + 1).astype(np.float64)
    result = []
    for spread in kernel_sigmas:
        norm = np.sum(np.exp(-axis * axis / (2.0 * spread * spread)))
        result.append(
            np.where(
                np.abs(offset) <= half_span,
                np.exp(-offset * offset / (2.0 * spread * spread)),
                0.0,
            )
            / norm
        )
    return np.stack(result)


def tap_pair(taps):
    high = taps.astype(jnp.bfloat16)
    low = (taps - high.astype(np.float64)).astype(jnp.bfloat16)
    return jnp.asarray(np.stack([high, low]))


def split(value):
    high = value.astype(jnp.bfloat16)
    return high, (value - high.astype(jnp.float32)).astype(jnp.bfloat16)


def products(pairs):
    total = None
    for left, right in pairs:
        term = jnp.dot(left, right, preferred_element_type=jnp.float32)
        total = term if total is None else total + term
    return total


def coadd_kernel(
    n, strips, bands,
    routes, slots, kernels, inverse, coefs, images, masks, across_in, down_in,
    coadd_out, detection_out,
    coadd, detection, across, down, pictures, bits_in, weights, raw, acc, planes, own_depth, raw_depth, table, raw_table,
    frame, result, depth_moving, moving, last_out, last_in, spilling, spilled,
    below, det_mine, det_theirs,
    taps_sem, in_sem, raw_send, raw_recv, table_sem, depth_send, depth_recv, send_sem, recv_sem,
    last_send, last_recv, spill_send, spill_recv, det_send, det_recv, out_sem,
):
    me = lax.axis_index("exp")
    strip = lax.axis_index("tile")
    band = lax.axis_index("band")
    held, block = pictures.shape[0], pictures.shape[1]
    span = block // CHUNKS
    rows_all, tile_cols = result.shape[1:]
    part = rows_all // PARTS
    half = tile_cols // 2
    at_left, at_right = me == 0, me == n - 1
    at_end = at_left | at_right
    gets_raw_left, gets_raw_right = me == 1, me == n - 2
    left_half = 2 * me < n - 1

    def input_copies(c):
        rows = pl.ds(pl.multiple_of(c * span, span), span)
        return (
            pltpu.make_async_copy(masks.at[:, rows], bits_in.at[:, rows], in_sem.at[c, 0]),
            pltpu.make_async_copy(images.at[:, rows], pictures.at[:, rows], in_sem.at[c, 1]),
        )

    for c in range(CHUNKS):
        for copy in input_copies(c):
            copy.start()

    taps_copies = (
        pltpu.make_async_copy(down_in, down, taps_sem.at[0]),
        pltpu.make_async_copy(across_in, across, taps_sem.at[1]),
    )
    for copy in taps_copies:
        copy.start()

    barrier = pltpu.get_barrier_semaphore()
    greet = [
        (strip > 0, {"tile": strip - 1}),
        (strip < strips - 1, {"tile": strip + 1}),
        (me > 0, {"exp": me - 1}),
        (me < n - 1, {"exp": me + 1}),
    ]
    peers = bands - 1
    for here, peer in greet:

        @pl.when(here)
        def _(peer=peer):
            pl.semaphore_signal(barrier, inc=1, device_id=peer, device_id_type=MESH)

        peers = peers + here.astype(jnp.int32)
    for j in range(1, bands):
        pl.semaphore_signal(
            barrier, inc=1, device_id={"band": lax.rem(band + j, bands)}, device_id_type=MESH
        )

    def last_of(entries, d, slot):
        return entries[held + (d + 1) * SLOTS + slot]

    inward = jnp.where(at_left, 1, n - 2)

    def raw_copy(c):
        return pltpu.make_async_remote_copy(
            src_ref=weights.at[c],
            dst_ref=raw.at[c],
            send_sem=raw_send.at[0],
            recv_sem=raw_recv.at[c],
            device_id={"exp": inward},
            device_id_type=MESH,
        )

    def table_copy():
        return pltpu.make_async_remote_copy(
            src_ref=table,
            dst_ref=raw_table,
            send_sem=table_sem.at[0],
            recv_sem=table_sem.at[1],
            device_id={"exp": inward},
            device_id_type=MESH,
        )

    def scaled_of(i, rows):
        bits = bits_in[i, rows]
        suspect = jnp.bitwise_and(bits, 1).astype(jnp.float32)
        usable = jnp.where(jnp.bitwise_and(bits, 6) == 6, 0.0, 1.0 - 0.5 * suspect)
        return usable * inverse[i]

    def weigh(c, carry):
        input_copies(c)[0].wait()
        rows = pl.ds(pl.multiple_of(c * span, span), span)
        for i in range(held):
            weights[c, i] = scaled_of(i, rows).astype(jnp.bfloat16)
        return carry

    weigh(0, 0)
    pl.semaphore_wait(barrier, peers)

    @pl.when(at_end)
    def _():
        raw_copy(0).start()

    keys = [routes[i] * SLOTS + slots[i] for i in range(held)]
    for i in range(held):
        before = held
        for j in range(i):
            before = jnp.where(keys[j] == keys[i], j, before)
        table[i] = jnp.int32(before)

    def note_last(key, carry):
        last = held
        for i in range(held):
            last = jnp.where(routes[i] * SLOTS + slots[i] == key - SLOTS, i, last)
        table[held + key] = last
        return carry

    lax.fori_loop(0, (n + 2) * SLOTS, note_last, 0)

    @pl.when(at_end)
    def _():
        table_copy().start()

    def weigh_and_send(c, carry):
        weigh(c, 0)

        @pl.when(at_end)
        def _():
            raw_copy(c).start()

        return carry

    lax.fori_loop(1, EARLY, weigh_and_send, 0)
    for c in range(EARLY, CHUNKS):
        weigh(c, 0)

    none = jnp.zeros((block, block), jnp.float32)
    for k in range(3):
        acc[held, k] = none
    for k in range(4):
        planes[held, k] = none.astype(jnp.bfloat16)
    own_depth[held] = none
    raw_depth[held] = none

    sends_spill = (strip < strips - 1, strip > 0)
    gets_spill = (strip > 0, strip < strips - 1)
    for side in range(2):

        @pl.when(jnp.logical_not(gets_spill[side]))
        def _(side=side):
            spilled[side] = jnp.zeros(spilled.shape[1:], spilled.dtype)


    def prepare(c, carry):
        input_copies(c)[1].wait()
        rows = pl.ds(pl.multiple_of(c * span, span), span)
        for i in range(held):
            scaled = scaled_of(i, rows)
            weighted = (
                (scaled * pictures[i, rows].astype(jnp.float32))
                .astype(jnp.bfloat16)
                .astype(jnp.float32)
            )
            before = table[i]
            which = kernels[i]
            own_depth[i, rows] = weights[c, i].astype(jnp.float32) + own_depth[before, rows]
            sums = []
            for k in range(3):
                value = coefs[k, which] * weighted + acc[before, k, rows]
                acc[i, k, rows] = value
                sums.append(value)
            planes[i, 0, rows], planes[i, 1, rows] = split(sums[0])
            planes[i, 2, rows] = sums[1].astype(jnp.bfloat16)
            planes[i, 3, rows] = sums[2].astype(jnp.bfloat16)

        return carry

    lax.fori_loop(0, CHUNKS, prepare, 0)

    for copy in taps_copies:
        copy.wait()

    def spill_copy(side, d):
        peer = strip + 1 if side == 0 else strip - 1
        return pltpu.make_async_remote_copy(
            src_ref=spilling.at[side, d],
            dst_ref=spilled.at[side, d],
            send_sem=spill_send.at[side],
            recv_sem=spill_recv.at[side, d],
            device_id={"tile": peer},
            device_id_type=MESH,
        )

    def correlate(d):
        for b in range(-1, BLOCK_COLS + 1):
            tile = d + b // BLOCK_COLS
            cols = slice((b + 1) * block, (b + 2) * block)
            for r in range(BLOCK_ROWS):
                which = last_of(table, tile, r * BLOCK_COLS + b % BLOCK_COLS)
                for k in range(4):
                    frame[k, r * block : (r + 1) * block, cols] = planes[which, k]
        first = (frame[0], frame[1])
        tall_high, tall_low = split(
            products(((down[0, 0], first[0]), (down[0, 0], first[1]), (down[1, 0], first[0])))
        )
        second = frame[2]
        tall_second = products(((down[0, 1], second), (down[1, 1], second))).astype(jnp.bfloat16)
        tall_third = products(((down[0, 2], frame[3]),)).astype(jnp.bfloat16)
        for h in range(2):
            cols = slice(h * half, h * half + half + 2 * block)
            total = products((
                (tall_high[:, cols], across[0, 0]),
                (tall_high[:, cols], across[1, 0]),
                (tall_low[:, cols], across[0, 0]),
                (tall_second[:, cols], across[0, 1]),
                (tall_second[:, cols], across[1, 1]),
                (tall_third[:, cols], across[0, 2]),
            ))
            out = slice(h * half, (h + 1) * half)
            result[d, :, out] = total[SPILL : SPILL + rows_all]
            spilling[0, d, :, out] = total[SPILL + rows_all :].astype(jnp.bfloat16)
            spilling[1, d, :, out] = total[0:SPILL].astype(jnp.bfloat16)
        for side in range(2):

            @pl.when(sends_spill[side])
            def _(side=side):
                spill_copy(side, d).start()

    def step(right, s):
        d = jnp.where(right, n - 1 - s, s)
        sends = jnp.where(right, d > me, d < me)
        gets = jnp.where(right, me > 0, me < n - 1)
        place = jnp.where(right, d, jnp.where(d == me - 1, n, d))
        return d, sends, gets, place, jnp.where(right, me + 1, me - 1)

    def arrived(ref, sems, place, c):
        pltpu.make_async_remote_copy(
            src_ref=ref.at[place, c],
            dst_ref=ref.at[place, c],
            send_sem=sems.at[place, c],
            recv_sem=sems.at[place, c],
            device_id={"band": lax.rem(band + 1, bands)},
            device_id_type=MESH,
        ).wait_recv()

    def depth_copy(right, s, c):
        d, _sends, _gets, place, target = step(right, s)
        return pltpu.make_async_remote_copy(
            src_ref=depth_moving.at[d, c],
            dst_ref=depth_moving.at[place, c],
            send_sem=depth_send.at[d],
            recv_sem=depth_recv.at[place, c],
            device_id={"exp": target},
            device_id_type=MESH,
        )

    def add_depth(d, c, extra):
        rows = pl.ds(pl.multiple_of(c * span, span), span)
        for r in range(BLOCK_ROWS):
            for b in range(BLOCK_COLS):
                slot = r * BLOCK_COLS + b
                cols = slice(b * block, (b + 1) * block)
                value = own_depth[last_of(table, d, slot), rows] + extra(r, slot, cols, rows)
                depth_moving[d, c, r, :, cols] = value.astype(jnp.bfloat16)

    def move_depth(right, s, c):
        d, sends, _gets, _place, _target = step(right, s)
        from_raw = jnp.where(right, gets_raw_left, gets_raw_right)

        @pl.when(sends & jnp.logical_not(at_end))
        def _():
            @pl.when(from_raw)
            def _():
                add_depth(
                    d, c,
                    lambda r, slot, cols, rows: raw_depth[last_of(raw_table, d, slot), rows],
                )

            @pl.when(jnp.logical_not(from_raw))
            def _():
                arrived(depth_moving, depth_recv, d, c)
                add_depth(
                    d, c,
                    lambda r, slot, cols, rows: depth_moving[d, c, r, :, cols].astype(jnp.float32),
                )

            depth_copy(right, s, c).start()

    def directions():
        return (left_half, jnp.logical_not(left_half))

    def lag(right):
        return LAG * jnp.where(right, me - 1, n - 2 - me)

    def take_raw(c):
        @pl.when(c == 0)
        def _():
            table_copy().wait_recv()

        raw_copy(c).wait_recv()
        rows = pl.ds(pl.multiple_of(c * span, span), span)
        for i in range(held):
            raw_depth[i, rows] = raw[c, i].astype(jnp.float32) + raw_depth[raw_table[i], rows]

    def complete(d):
        for side in range(2):

            @pl.when(gets_spill[side])
            def _(side=side):
                spill_copy(side, d).wait_recv()

        low = rows_all - SPILL
        result[d, 0:SPILL] += spilled[0, d].astype(jnp.float32)
        result[d, low:] += spilled[1, d].astype(jnp.float32)

    def pick(i):
        down_from = n - 1 - i
        right = jnp.where(down_from > me, down_from, down_from - 1)
        left = jnp.where(i < me, i, i + 1)
        return jnp.where(i == n - 1, me, jnp.where(left_half, right, left))

    def part_copy(right, s, q):
        d, _sends, _gets, place, target = step(right, s)
        return pltpu.make_async_remote_copy(
            src_ref=moving.at[d, q],
            dst_ref=moving.at[place, q],
            send_sem=send_sem.at[d],
            recv_sem=recv_sem.at[place, q],
            device_id={"exp": target},
            device_id_type=MESH,
        )

    def last_copy(q):
        target = jnp.where(me == n - 2, n - 1, 0)
        return pltpu.make_async_remote_copy(
            src_ref=last_out.at[q],
            dst_ref=last_in.at[q],
            send_sem=last_send.at[0],
            recv_sem=last_recv.at[q],
            device_id={"exp": target},
            device_id_type=MESH,
        )

    def part_rows(q):
        return pl.ds(pl.multiple_of(q * part, part), part)

    def move_first(i):
        s = i

        def one(q, carry):
            d = step(at_left, s)[0]
            moving[d, q] = result[d, part_rows(q)].astype(jnp.bfloat16)
            part_copy(at_left, s, q).start()
            return carry

        lax.fori_loop(0, PARTS, one, 0)

    def move_part(right, s, q):
        d, sends, _gets, _place, _target = step(right, s)
        wide = jnp.where(right, me == n - 2, me == 1) & (s == 0) & (q < WIDE)

        @pl.when(sends & jnp.logical_not(at_end))
        def _():
            arrived(moving, recv_sem, d, q)
            value = moving[d, q].astype(jnp.float32) + result[d, part_rows(q)]

            @pl.when(wide)
            def _():
                last_out[q] = value
                last_copy(q).start()

            @pl.when(jnp.logical_not(wide))
            def _():
                moving[d, q] = value.astype(jnp.bfloat16)
                part_copy(right, s, q).start()

    early, late = EARLY * STRIDE, (CHUNKS - EARLY) * STRIDE
    events = early + late + (n - 1) * PARTS

    def slot(t, carry):
        for right in directions():
            e = t - lag(right)
            in_early = e < early
            in_late = (e >= early + PARTS) & (e < early + PARTS + late)
            of_depth = jnp.where(in_early, e, e - PARTS)
            is_depth = (e >= 0) & (in_early | in_late)

            @pl.when(is_depth & (lax.rem(of_depth, STRIDE) == 0))
            def _(right=right, of_depth=of_depth):
                c = of_depth // STRIDE

                @pl.when(jnp.where(right, gets_raw_left, gets_raw_right))
                def _():
                    take_raw(c)

                def one(s, carry):
                    move_depth(right, s, c)
                    return carry

                lax.fori_loop(0, n - 1, one, 0)

            @pl.when((e >= early) & (e < events) & jnp.logical_not(is_depth))
            def _(right=right, e=e):
                i = jnp.where(e < early + PARTS, e - early, e - early - late)
                move_part(right, i // PARTS, lax.rem(i, PARTS))

        return carry

    def turn(i, carry):
        correlate(pick(i))

        @pl.when(i > 0)
        def _():
            complete(pick(i - 1))

            @pl.when(at_end)
            def _():
                move_first(i - 1)

                @pl.when(i == 1)
                def _():
                    for c in range(EARLY, CHUNKS):
                        raw_copy(c).start()

        @pl.when((i < EARLY) & jnp.logical_not(at_end))
        def _():
            lax.fori_loop(i * STRIDE, (i + 1) * STRIDE, slot, 0)

        return carry

    lax.fori_loop(0, n, turn, 0)

    @pl.when(jnp.logical_not(at_end))
    def _():
        lax.fori_loop(early, events + LAG * (n - 3), slot, 0)

    complete(me)

    def bottom(c, carry):
        chunk_rows = pl.ds(pl.multiple_of(c * span, span), span)
        for r in range(BLOCK_ROWS):
            for b in range(BLOCK_COLS):
                slot = r * BLOCK_COLS + b
                cols = slice(b * block, (b + 1) * block)
                rows = pl.ds(pl.multiple_of(r * block + c * span, span), span)
                below[rows, cols] = 1.0 + own_depth[last_of(table, me, slot), chunk_rows]

        @pl.when(gets_raw_left | gets_raw_right)
        def _():
            for r in range(BLOCK_ROWS):
                for b in range(BLOCK_COLS):
                    slot = r * BLOCK_COLS + b
                    cols = slice(b * block, (b + 1) * block)
                    rows = pl.ds(pl.multiple_of(r * block + c * span, span), span)
                    below[rows, cols] += raw_depth[last_of(raw_table, me, slot), chunk_rows]

        for has, place in (
            ((me > 1), me),
            ((me < n - 2), n),
        ):

            @pl.when(has)
            def _(place=place):
                arrived(depth_moving, depth_recv, place, c)
                for r in range(BLOCK_ROWS):
                    rows = pl.ds(pl.multiple_of(r * block + c * span, span), span)
                    below[rows] += depth_moving[place, c, r].astype(jnp.float32)

        return carry

    lax.fori_loop(0, CHUNKS, bottom, 0)

    def det_copy(j, q):
        return pltpu.make_async_remote_copy(
            src_ref=det_mine.at[part_rows(q)],
            dst_ref=det_theirs.at[j - 1, part_rows(q)],
            send_sem=det_send.at[j - 1],
            recv_sem=det_recv.at[j - 1, q],
            device_id={"band": lax.rem(band + j, bands)},
            device_id_type=MESH,
        )

    def out_copy(k, q):
        rows = part_rows(q)
        if k == 0:
            return pltpu.make_async_copy(coadd.at[rows], coadd_out.at[rows], out_sem.at[k])
        return pltpu.make_async_copy(detection.at[rows], detection_out.at[rows], out_sem.at[k])

    def finish(q, carry):
        rows = part_rows(q)

        @pl.when(at_end & (q < WIDE))
        def _():
            last_copy(q).wait_recv()
            result[me, rows] += last_in[q]

        @pl.when(at_end & (q >= WIDE))
        def _():
            place = jnp.where(at_left, n, me)
            arrived(moving, recv_sem, place, q)
            result[me, rows] += moving[place, q].astype(jnp.float32)

        @pl.when(jnp.logical_not(at_end))
        def _():
            arrived(moving, recv_sem, me, q)
            arrived(moving, recv_sem, n, q)
            result[me, rows] += moving[me, q].astype(jnp.float32) + moving[n, q].astype(
                jnp.float32
            )

        value = result[me, rows] / below[rows]
        coadd[rows] = value
        out_copy(0, q).start()
        det_mine[rows] = value * value * below[rows]
        for j in range(1, bands):
            det_copy(j, q).start()
        return carry

    lax.fori_loop(0, PARTS, finish, 0)

    def sent(ref, sem):
        pltpu.make_async_remote_copy(
            src_ref=ref,
            dst_ref=ref,
            send_sem=sem,
            recv_sem=sem,
            device_id={"band": lax.rem(band + 1, bands)},
            device_id_type=MESH,
        ).wait_send()

    @pl.when(at_end)
    def _():
        table_copy().wait_send()
        sent(weights, raw_send.at[0])

    def drain(s, carry):
        for right in directions():
            d, sends, _gets, _place, _target = step(right, s)
            to_end = jnp.where(right, me == n - 2, me == 1) & (s == 0)

            @pl.when(sends & jnp.logical_not(at_end))
            def _(d=d):
                sent(depth_moving.at[d], depth_send.at[d])

            @pl.when(sends & to_end)
            def _(d=d):
                sent(last_out, last_send.at[0])
                sent(moving.at[d, pl.ds(WIDE, PARTS - WIDE)], send_sem.at[d])

            @pl.when(sends & jnp.logical_not(to_end))
            def _(d=d):
                sent(moving.at[d], send_sem.at[d])

        return carry

    lax.fori_loop(0, n - 1, drain, 0)

    for side in range(2):

        @pl.when(sends_spill[side])
        def _(side=side):
            sent(spilling.at[side], spill_send.at[side])

    def combine(q, carry):
        rows = part_rows(q)
        value = det_mine[rows]
        for j in range(1, bands):
            det_copy(j, q).wait_recv()
            value += det_theirs[j - 1, rows]
        detection[rows] = value
        out_copy(1, q).start()
        return carry

    lax.fori_loop(0, PARTS, combine, 0)

    for j in range(1, bands):
        sent(det_mine, det_send.at[j - 1])
    pltpu.make_async_copy(coadd, coadd_out, out_sem.at[0]).wait()
    pltpu.make_async_copy(detection, detection_out, out_sem.at[1]).wait()


def local(sizes, images, mask_bits, inv_var, routes, block_slot, kernel_index, coefficients):
    n, strips, bands = sizes["exp"], sizes["tile"], sizes["band"]
    held, block = images.shape[2:4]
    tile_rows = BLOCK_ROWS * block
    tile_cols = BLOCK_COLS * block
    half = tile_cols // 2
    span = block // CHUNKS
    part = tile_rows // PARTS
    entries = pl.cdiv(held + (n + 2) * SLOTS, 128) * 128
    across = tap_pair(tap_matrix(2 * half, half, block))
    down = tap_pair(tap_matrix(tile_rows + 2 * SPILL, tile_rows, SPILL))
    smem = pl.BlockSpec(memory_space=pltpu.SMEM)
    vmem = pl.BlockSpec(memory_space=pltpu.VMEM)
    anywhere = pl.BlockSpec(memory_space=pltpu.HBM)
    whole = jax.ShapeDtypeStruct((tile_rows, tile_cols), jnp.float32)
    bf16, f32 = jnp.bfloat16, jnp.float32
    dma = pltpu.SemaphoreType.DMA
    scratch = [
        pltpu.VMEM((tile_rows, tile_cols), f32),
        pltpu.VMEM((tile_rows, tile_cols), f32),
        pltpu.VMEM(across.shape, bf16),
        pltpu.VMEM(down.shape, bf16),
        pltpu.VMEM((held, block, block), bf16),
        pltpu.VMEM((held, block, block), jnp.int32),
        pltpu.VMEM((CHUNKS, held, span, block), bf16),
        pltpu.VMEM((CHUNKS, held, span, block), bf16),
        pltpu.VMEM((held + 1, 3, block, block), f32),
        pltpu.VMEM((held + 1, 4, block, block), bf16),
        pltpu.VMEM((held + 1, block, block), f32),
        pltpu.VMEM((held + 1, block, block), f32),
        pltpu.SMEM((entries,), jnp.int32),
        pltpu.SMEM((entries,), jnp.int32),
        pltpu.VMEM((4, tile_rows, tile_cols + 2 * block), bf16),
        pltpu.VMEM((n, tile_rows, tile_cols), f32),
        pltpu.VMEM((n + 1, CHUNKS, BLOCK_ROWS, span, tile_cols), bf16),
        pltpu.VMEM((n + 1, PARTS, part, tile_cols), bf16),
        pltpu.VMEM((WIDE, part, tile_cols), f32),
        pltpu.VMEM((WIDE, part, tile_cols), f32),
        pltpu.VMEM((2, n, SPILL, tile_cols), bf16),
        pltpu.VMEM((2, n, SPILL, tile_cols), bf16),
        pltpu.VMEM((tile_rows, tile_cols), f32),
        pltpu.VMEM((tile_rows, tile_cols), f32),
        pltpu.VMEM((bands - 1, tile_rows, tile_cols), f32),
        dma((2,)),
        dma((CHUNKS, 2)),
        dma((1,)),
        dma((CHUNKS,)),
        dma((2,)),
        dma((n,)),
        dma((n + 1, CHUNKS)),
        dma((n,)),
        dma((n + 1, PARTS)),
        dma((1,)),
        dma((WIDE,)),
        dma((2,)),
        dma((2, n)),
        dma((bands - 1,)),
        dma((bands - 1, PARTS)),
        dma((2,)),
    ]
    held_bytes = sum(
        int(np.prod(x.shape)) * jnp.dtype(x.dtype).itemsize
        for x in scratch
        if x.memory_space == pltpu.VMEM
    )
    limit = min(held_bytes + (16 << 20), 60 * 1024 * 1024)
    coadd, detection = pl.pallas_call(
        functools.partial(coadd_kernel, n, strips, bands),
        out_shape=(whole, whole),
        in_specs=[smem] * 5 + [anywhere] * 4,
        out_specs=(pl.BlockSpec(memory_space=pl.ANY),) * 2,
        scratch_shapes=scratch,
        compiler_params=pltpu.CompilerParams(collective_id=0, has_side_effects=True, vmem_limit_bytes=limit),
        name="coadd",
    )(*[
        pltpu.with_memory_space_constraint(x, pltpu.HBM)
        for x in (
            routes[0, 0, :, 0], block_slot[0, 0], kernel_index[0, 0], inv_var[0, 0],
            coefficients.T, images[0, 0], mask_bits[0, 0], across, down,
        )
    ])
    return coadd[None], detection


def solution(mesh):
    return jax.shard_map(
        functools.partial(local, dict(mesh.shape)),
        mesh=mesh,
        in_specs=(
            P(("patch", "band"), "tile", "exp", None, None),
            P(("patch", "band"), "tile", "exp", None, None),
            P(("patch", "band"), "tile", "exp"),
            P(("patch", "band"), "tile", "exp", None),
            P(("patch", "band"), "tile", "exp"),
            P(("patch", "band"), "tile", "exp"),
            P(),
        ),
        out_specs=(P(("patch", "band"), "tile", "exp"), P(("patch", "tile"), "exp")),
        check_vma=False,
    )
```

```python
import functools

import jax
import jax.numpy as jnp
import numpy as np
from jax import lax
from jax.experimental import pallas as pl
from jax.experimental.pallas import tpu as pltpu
from jax.sharding import PartitionSpec as P

TAPS = 41
BLOCK_ROWS = 2
BLOCK_COLS = 4
SLOTS = BLOCK_ROWS * BLOCK_COLS
SPILL = 24
CHUNKS = 4
PARTS = 8
STRIDE = 4
EARLY = 3
WIDE = 3
HANDS = 1
LAG = 6

kernel_sigmas = (1.0, 2.5, 6.0)
MESH = pl.DeviceIdType.MESH


def tap_matrix(rows, cols, shift):
    half_span = TAPS // 2
    offset = np.arange(rows)[:, None] - np.arange(cols)[None, :] - shift
    axis = np.arange(-half_span, half_span + 1).astype(np.float64)
    result = []
    for spread in kernel_sigmas:
        norm = np.sum(np.exp(-axis * axis / (2.0 * spread * spread)))
        result.append(
            np.where(
                np.abs(offset) <= half_span,
                np.exp(-offset * offset / (2.0 * spread * spread)),
                0.0,
            )
            / norm
        )
    return np.stack(result)


def tap_pair(taps):
    high = taps.astype(jnp.bfloat16)
    low = (taps - high.astype(np.float64)).astype(jnp.bfloat16)
    return jnp.asarray(np.stack([high, low]))


def split(value):
    high = value.astype(jnp.bfloat16)
    return high, (value - high.astype(jnp.float32)).astype(jnp.bfloat16)


def products(pairs):
    total = None
    for left, right in pairs:
        term = jnp.dot(left, right, preferred_element_type=jnp.float32)
        total = term if total is None else total + term
    return total


def coadd_kernel(
    n, strips, bands,
    routes, slots, kernels, inverse, coefs, images, masks, across_in, down_in,
    coadd_out, detection_out,
    coadd, detection, across, down, pictures, bits_in, weights, raw, acc, planes, own_depth, raw_depth, table, raw_table,
    frame, result, depth_moving, moving, last_out, last_in, spilling, spilled,
    below, det_mine, det_theirs,
    taps_sem, in_sem, raw_send, raw_recv, table_sem, depth_send, depth_recv, send_sem, recv_sem,
    last_send, last_recv, spill_send, spill_recv, det_send, det_recv, out_sem,
):
    me = lax.axis_index("exp")
    strip = lax.axis_index("tile")
    band = lax.axis_index("band")
    held, block = pictures.shape[0], pictures.shape[1]
    span = block // CHUNKS
    rows_all, tile_cols = result.shape[1:]
    part = rows_all // PARTS
    half = tile_cols // 2
    at_left, at_right = me == 0, me == n - 1
    at_end = at_left | at_right
    gets_raw_left, gets_raw_right = me == 1, me == n - 2
    left_half = 2 * me < n - 1

    def input_copies(c):
        rows = pl.ds(pl.multiple_of(c * span, span), span)
        return (
            pltpu.make_async_copy(masks.at[:, rows], bits_in.at[:, rows], in_sem.at[c, 0]),
            pltpu.make_async_copy(images.at[:, rows], pictures.at[:, rows], in_sem.at[c, 1]),
        )

    for c in range(CHUNKS):
        for copy in input_copies(c):
            copy.start()

    taps_copies = (
        pltpu.make_async_copy(down_in, down, taps_sem.at[0]),
        pltpu.make_async_copy(across_in, across, taps_sem.at[1]),
    )
    for copy in taps_copies:
        copy.start()

    barrier = pltpu.get_barrier_semaphore()
    greet = [
        (strip > 0, {"tile": strip - 1}),
        (strip < strips - 1, {"tile": strip + 1}),
        (me > 0, {"exp": me - 1}),
        (me < n - 1, {"exp": me + 1}),
    ]
    peers = bands - 1
    for here, peer in greet:

        @pl.when(here)
        def _(peer=peer):
            pl.semaphore_signal(barrier, inc=1, device_id=peer, device_id_type=MESH)

        peers = peers + here.astype(jnp.int32)
    for j in range(1, bands):
        pl.semaphore_signal(
            barrier, inc=1, device_id={"band": lax.rem(band + j, bands)}, device_id_type=MESH
        )

    def last_of(entries, d, slot):
        return entries[held + (d + 1) * SLOTS + slot]

    inward = jnp.where(at_left, 1, n - 2)

    def raw_copy(c):
        return pltpu.make_async_remote_copy(
            src_ref=weights.at[c],
            dst_ref=raw.at[c],
            send_sem=raw_send.at[0],
            recv_sem=raw_recv.at[c],
            device_id={"exp": inward},
            device_id_type=MESH,
        )

    def table_copy():
        return pltpu.make_async_remote_copy(
            src_ref=table,
            dst_ref=raw_table,
            send_sem=table_sem.at[0],
            recv_sem=table_sem.at[1],
            device_id={"exp": inward},
            device_id_type=MESH,
        )

    def scaled_of(i, rows):
        bits = bits_in[i, rows]
        suspect = jnp.bitwise_and(bits, 1).astype(jnp.float32)
        usable = jnp.where(jnp.bitwise_and(bits, 6) == 6, 0.0, 1.0 - 0.5 * suspect)
        return usable * inverse[i]

    def weigh(c, carry):
        input_copies(c)[0].wait()
        rows = pl.ds(pl.multiple_of(c * span, span), span)
        for i in range(held):
            weights[c, i] = scaled_of(i, rows).astype(jnp.bfloat16)
        return carry

    weigh(0, 0)
    pl.semaphore_wait(barrier, peers)

    @pl.when(at_end)
    def _():
        raw_copy(0).start()

    keys = [routes[i] * SLOTS + slots[i] for i in range(held)]
    for i in range(held):
        before = held
        for j in range(i):
            before = jnp.where(keys[j] == keys[i], j, before)
        table[i] = jnp.int32(before)

    def note_last(key, carry):
        last = held
        for i in range(held):
            last = jnp.where(routes[i] * SLOTS + slots[i] == key - SLOTS, i, last)
        table[held + key] = last
        return carry

    lax.fori_loop(0, (n + 2) * SLOTS, note_last, 0)

    @pl.when(at_end)
    def _():
        table_copy().start()

    def weigh_and_send(c, carry):
        weigh(c, 0)

        @pl.when(at_end)
        def _():
            raw_copy(c).start()

        return carry

    lax.fori_loop(1, EARLY, weigh_and_send, 0)
    for c in range(EARLY, CHUNKS):
        weigh(c, 0)

    none = jnp.zeros((block, block), jnp.float32)
    for k in range(3):
        acc[held, k] = none
    for k in range(4):
        planes[held, k] = none.astype(jnp.bfloat16)
    own_depth[held] = none
    raw_depth[held] = none

    sends_spill = (strip < strips - 1, strip > 0)
    gets_spill = (strip > 0, strip < strips - 1)
    for side in range(2):

        @pl.when(jnp.logical_not(gets_spill[side]))
        def _(side=side):
            spilled[side] = jnp.zeros(spilled.shape[1:], spilled.dtype)


    def prepare(c, carry):
        input_copies(c)[1].wait()
        rows = pl.ds(pl.multiple_of(c * span, span), span)
        for i in range(held):
            scaled = scaled_of(i, rows)
            weighted = (
                (scaled * pictures[i, rows].astype(jnp.float32))
                .astype(jnp.bfloat16)
                .astype(jnp.float32)
            )
            before = table[i]
            which = kernels[i]
            own_depth[i, rows] = weights[c, i].astype(jnp.float32) + own_depth[before, rows]
            sums = []
            for k in range(3):
                value = coefs[k, which] * weighted + acc[before, k, rows]
                acc[i, k, rows] = value
                sums.append(value)
            planes[i, 0, rows], planes[i, 1, rows] = split(sums[0])
            planes[i, 2, rows] = sums[1].astype(jnp.bfloat16)
            planes[i, 3, rows] = sums[2].astype(jnp.bfloat16)

        return carry

    lax.fori_loop(0, CHUNKS, prepare, 0)

    for copy in taps_copies:
        copy.wait()

    def spill_copy(side, d):
        peer = strip + 1 if side == 0 else strip - 1
        return pltpu.make_async_remote_copy(
            src_ref=spilling.at[side, d],
            dst_ref=spilled.at[side, d],
            send_sem=spill_send.at[side],
            recv_sem=spill_recv.at[side, d],
            device_id={"tile": peer},
            device_id_type=MESH,
        )

    def correlate(d):
        for b in range(-1, BLOCK_COLS + 1):
            tile = d + b // BLOCK_COLS
            cols = slice((b + 1) * block, (b + 2) * block)
            for r in range(BLOCK_ROWS):
                which = last_of(table, tile, r * BLOCK_COLS + b % BLOCK_COLS)
                for k in range(4):
                    frame[k, r * block : (r + 1) * block, cols] = planes[which, k]
        first = (frame[0], frame[1])
        tall_high, tall_low = split(
            products(((down[0, 0], first[0]), (down[0, 0], first[1]), (down[1, 0], first[0])))
        )
        second = frame[2]
        tall_second = products(((down[0, 1], second), (down[1, 1], second))).astype(jnp.bfloat16)
        tall_third = products(((down[0, 2], frame[3]),)).astype(jnp.bfloat16)
        for h in range(2):
            cols = slice(h * half, h * half + half + 2 * block)
            total = products((
                (tall_high[:, cols], across[0, 0]),
                (tall_high[:, cols], across[1, 0]),
                (tall_low[:, cols], across[0, 0]),
                (tall_second[:, cols], across[0, 1]),
                (tall_second[:, cols], across[1, 1]),
                (tall_third[:, cols], across[0, 2]),
            ))
            out = slice(h * half, (h + 1) * half)
            result[d, :, out] = total[SPILL : SPILL + rows_all]
            spilling[0, d, :, out] = total[SPILL + rows_all :].astype(jnp.bfloat16)
            spilling[1, d, :, out] = total[0:SPILL].astype(jnp.bfloat16)
        for side in range(2):

            @pl.when(sends_spill[side])
            def _(side=side):
                spill_copy(side, d).start()

    def step(right, s):
        d = jnp.where(right, n - 1 - s, s)
        sends = jnp.where(right, d > me, d < me)
        gets = jnp.where(right, me > 0, me < n - 1)
        place = jnp.where(right, d, jnp.where(d == me - 1, n, d))
        return d, sends, gets, place, jnp.where(right, me + 1, me - 1)

    def arrived(ref, sems, place, c):
        pltpu.make_async_remote_copy(
            src_ref=ref.at[place, c],
            dst_ref=ref.at[place, c],
            send_sem=sems.at[place, c],
            recv_sem=sems.at[place, c],
            device_id={"band": lax.rem(band + 1, bands)},
            device_id_type=MESH,
        ).wait_recv()

    def depth_copy(right, s, c):
        d, _sends, _gets, place, target = step(right, s)
        return pltpu.make_async_remote_copy(
            src_ref=depth_moving.at[d, c],
            dst_ref=depth_moving.at[place, c],
            send_sem=depth_send.at[d],
            recv_sem=depth_recv.at[place, c],
            device_id={"exp": target},
            device_id_type=MESH,
        )

    def add_depth(d, c, extra):
        rows = pl.ds(pl.multiple_of(c * span, span), span)
        for r in range(BLOCK_ROWS):
            for b in range(BLOCK_COLS):
                slot = r * BLOCK_COLS + b
                cols = slice(b * block, (b + 1) * block)
                value = own_depth[last_of(table, d, slot), rows] + extra(r, slot, cols, rows)
                depth_moving[d, c, r, :, cols] = value.astype(jnp.bfloat16)

    def move_depth(right, s, c):
        d, sends, _gets, _place, _target = step(right, s)
        from_raw = jnp.where(right, gets_raw_left, gets_raw_right)

        @pl.when(sends & jnp.logical_not(at_end))
        def _():
            @pl.when(from_raw)
            def _():
                add_depth(
                    d, c,
                    lambda r, slot, cols, rows: raw_depth[last_of(raw_table, d, slot), rows],
                )

            @pl.when(jnp.logical_not(from_raw))
            def _():
                arrived(depth_moving, depth_recv, d, c)
                add_depth(
                    d, c,
                    lambda r, slot, cols, rows: depth_moving[d, c, r, :, cols].astype(jnp.float32),
                )

            depth_copy(right, s, c).start()

    def directions():
        return (left_half, jnp.logical_not(left_half))

    def lag(right):
        return LAG * jnp.where(right, me - 1, n - 2 - me)

    def take_raw(c):
        @pl.when(c == 0)
        def _():
            table_copy().wait_recv()

        raw_copy(c).wait_recv()
        rows = pl.ds(pl.multiple_of(c * span, span), span)
        for i in range(held):
            raw_depth[i, rows] = raw[c, i].astype(jnp.float32) + raw_depth[raw_table[i], rows]

    def complete(d):
        for side in range(2):

            @pl.when(gets_spill[side])
            def _(side=side):
                spill_copy(side, d).wait_recv()

        low = rows_all - SPILL
        result[d, 0:SPILL] += spilled[0, d].astype(jnp.float32)
        result[d, low:] += spilled[1, d].astype(jnp.float32)

    def pick(i):
        down_from = n - 1 - i
        right = jnp.where(down_from > me, down_from, down_from - 1)
        left = jnp.where(i < me, i, i + 1)
        return jnp.where(i == n - 1, me, jnp.where(left_half, right, left))

    def part_copy(right, s, q):
        d, _sends, _gets, place, target = step(right, s)
        return pltpu.make_async_remote_copy(
            src_ref=moving.at[d, q],
            dst_ref=moving.at[place, q],
            send_sem=send_sem.at[d],
            recv_sem=recv_sem.at[place, q],
            device_id={"exp": target},
            device_id_type=MESH,
        )

    def last_copy(q):
        target = jnp.where(me == n - 2, n - 1, 0)
        return pltpu.make_async_remote_copy(
            src_ref=last_out.at[q],
            dst_ref=last_in.at[q],
            send_sem=last_send.at[0],
            recv_sem=last_recv.at[q],
            device_id={"exp": target},
            device_id_type=MESH,
        )

    def part_rows(q):
        return pl.ds(pl.multiple_of(q * part, part), part)

    def move_first(i):
        s = i

        def one(q, carry):
            d = step(at_left, s)[0]
            moving[d, q] = result[d, part_rows(q)].astype(jnp.bfloat16)
            part_copy(at_left, s, q).start()
            return carry

        lax.fori_loop(0, PARTS, one, 0)

    def move_part(right, s, q):
        d, sends, _gets, _place, _target = step(right, s)
        wide = jnp.where(right, me == n - 2, me == 1) & (s == 0) & (q < WIDE)

        @pl.when(sends & jnp.logical_not(at_end))
        def _():
            arrived(moving, recv_sem, d, q)
            value = moving[d, q].astype(jnp.float32) + result[d, part_rows(q)]

            @pl.when(wide)
            def _():
                last_out[q] = value
                last_copy(q).start()

            @pl.when(jnp.logical_not(wide))
            def _():
                moving[d, q] = value.astype(jnp.bfloat16)
                part_copy(right, s, q).start()

    early, late = EARLY * STRIDE, (CHUNKS - EARLY) * STRIDE
    events = early + late + (n - 1) * PARTS

    def slot(t, carry):
        for right in directions():
            e = t - lag(right)
            in_early = e < early
            in_late = (e >= early + PARTS) & (e < early + PARTS + late)
            of_depth = jnp.where(in_early, e, e - PARTS)
            is_depth = (e >= 0) & (in_early | in_late)

            @pl.when(is_depth & (lax.rem(of_depth, STRIDE) == 0))
            def _(right=right, of_depth=of_depth):
                c = of_depth // STRIDE

                @pl.when(jnp.where(right, gets_raw_left, gets_raw_right))
                def _():
                    take_raw(c)

                def one(s, carry):
                    move_depth(right, s, c)
                    return carry

                lax.fori_loop(0, n - 1, one, 0)

            @pl.when((e >= early) & (e < events) & jnp.logical_not(is_depth))
            def _(right=right, e=e):
                i = jnp.where(e < early + PARTS, e - early, e - early - late)
                move_part(right, i // PARTS, lax.rem(i, PARTS))

        return carry

    def turn(i, carry):
        correlate(pick(i))

        @pl.when(i > 0)
        def _():
            complete(pick(i - 1))

            @pl.when(at_end)
            def _():
                move_first(i - 1)

                @pl.when(i == 1)
                def _():
                    for c in range(EARLY, CHUNKS):
                        raw_copy(c).start()

        @pl.when((i < EARLY) & jnp.logical_not(at_end))
        def _():
            lax.fori_loop(i * STRIDE, (i + 1) * STRIDE, slot, 0)

        return carry

    lax.fori_loop(0, n, turn, 0)

    @pl.when(jnp.logical_not(at_end))
    def _():
        lax.fori_loop(early, events + LAG * (n - 3), slot, 0)

    complete(me)

    def bottom(c, carry):
        chunk_rows = pl.ds(pl.multiple_of(c * span, span), span)
        for r in range(BLOCK_ROWS):
            for b in range(BLOCK_COLS):
                slot = r * BLOCK_COLS + b
                cols = slice(b * block, (b + 1) * block)
                rows = pl.ds(pl.multiple_of(r * block + c * span, span), span)
                below[rows, cols] = 1.0 + own_depth[last_of(table, me, slot), chunk_rows]

        @pl.when(gets_raw_left | gets_raw_right)
        def _():
            for r in range(BLOCK_ROWS):
                for b in range(BLOCK_COLS):
                    slot = r * BLOCK_COLS + b
                    cols = slice(b * block, (b + 1) * block)
                    rows = pl.ds(pl.multiple_of(r * block + c * span, span), span)
                    below[rows, cols] += raw_depth[last_of(raw_table, me, slot), chunk_rows]

        for has, place in (
            ((me > 1), me),
            ((me < n - 2), n),
        ):

            @pl.when(has)
            def _(place=place):
                arrived(depth_moving, depth_recv, place, c)
                for r in range(BLOCK_ROWS):
                    rows = pl.ds(pl.multiple_of(r * block + c * span, span), span)
                    below[rows] += depth_moving[place, c, r].astype(jnp.float32)

        return carry

    lax.fori_loop(0, CHUNKS, bottom, 0)

    def det_copy(j, q):
        return pltpu.make_async_remote_copy(
            src_ref=det_mine.at[part_rows(q)],
            dst_ref=det_theirs.at[j - 1, part_rows(q)],
            send_sem=det_send.at[j - 1],
            recv_sem=det_recv.at[j - 1, q],
            device_id={"band": lax.rem(band + j, bands)},
            device_id_type=MESH,
        )

    def out_copy(k, q):
        rows = part_rows(q)
        if k == 0:
            return pltpu.make_async_copy(coadd.at[rows], coadd_out.at[rows], out_sem.at[k])
        return pltpu.make_async_copy(detection.at[rows], detection_out.at[rows], out_sem.at[k])

    def finish(q, carry):
        rows = part_rows(q)

        @pl.when(at_end & (q < WIDE))
        def _():
            last_copy(q).wait_recv()
            result[me, rows] += last_in[q]

        @pl.when(at_end & (q >= WIDE))
        def _():
            place = jnp.where(at_left, n, me)
            arrived(moving, recv_sem, place, q)
            result[me, rows] += moving[place, q].astype(jnp.float32)

        @pl.when(jnp.logical_not(at_end))
        def _():
            arrived(moving, recv_sem, me, q)
            arrived(moving, recv_sem, n, q)
            result[me, rows] += moving[me, q].astype(jnp.float32) + moving[n, q].astype(
                jnp.float32
            )

        value = result[me, rows] / below[rows]
        coadd[rows] = value
        out_copy(0, q).start()
        det_mine[rows] = value * value * below[rows]
        for j in range(1, bands):
            det_copy(j, q).start()
        return carry

    lax.fori_loop(0, PARTS, finish, 0)

    def sent(ref, sem):
        pltpu.make_async_remote_copy(
            src_ref=ref,
            dst_ref=ref,
            send_sem=sem,
            recv_sem=sem,
            device_id={"band": lax.rem(band + 1, bands)},
            device_id_type=MESH,
        ).wait_send()

    @pl.when(at_end)
    def _():
        table_copy().wait_send()
        sent(weights, raw_send.at[0])

    def drain(s, carry):
        for right in directions():
            d, sends, _gets, _place, _target = step(right, s)
            to_end = jnp.where(right, me == n - 2, me == 1) & (s == 0)

            @pl.when(sends & jnp.logical_not(at_end))
            def _(d=d):
                sent(depth_moving.at[d], depth_send.at[d])

            @pl.when(sends & to_end)
            def _(d=d):
                sent(last_out, last_send.at[0])
                sent(moving.at[d, pl.ds(WIDE, PARTS - WIDE)], send_sem.at[d])

            @pl.when(sends & jnp.logical_not(to_end))
            def _(d=d):
                sent(moving.at[d], send_sem.at[d])

        return carry

    lax.fori_loop(0, n - 1, drain, 0)

    for side in range(2):

        @pl.when(sends_spill[side])
        def _(side=side):
            sent(spilling.at[side], spill_send.at[side])

    def combine(q, carry):
        rows = part_rows(q)
        value = det_mine[rows]
        for j in range(1, bands):
            det_copy(j, q).wait_recv()
            value += det_theirs[j - 1, rows]
        detection[rows] = value
        out_copy(1, q).start()
        return carry

    lax.fori_loop(0, PARTS, combine, 0)

    for j in range(1, bands):
        sent(det_mine, det_send.at[j - 1])
    pltpu.make_async_copy(coadd, coadd_out, out_sem.at[0]).wait()
    pltpu.make_async_copy(detection, detection_out, out_sem.at[1]).wait()


def hand_out_kernel(coadd, detection, coadd_out, detection_out, sem):
    rows = coadd.shape[0] // HANDS
    copies = []
    for q in range(HANDS):
        part = pl.ds(q * rows, rows)
        for k, (src, dst) in enumerate(((coadd, coadd_out), (detection, detection_out))):
            copies.append(pltpu.make_async_copy(src.at[part], dst.at[part], sem.at[k, q]))
    for copy in copies:
        copy.start()
    for copy in copies:
        copy.wait()


def local(sizes, images, mask_bits, inv_var, routes, block_slot, kernel_index, coefficients):
    n, strips, bands = sizes["exp"], sizes["tile"], sizes["band"]
    held, block = images.shape[2:4]
    tile_rows = BLOCK_ROWS * block
    tile_cols = BLOCK_COLS * block
    half = tile_cols // 2
    span = block // CHUNKS
    part = tile_rows // PARTS
    entries = pl.cdiv(held + (n + 2) * SLOTS, 128) * 128
    across = tap_pair(tap_matrix(2 * half, half, block))
    down = tap_pair(tap_matrix(tile_rows + 2 * SPILL, tile_rows, SPILL))
    smem = pl.BlockSpec(memory_space=pltpu.SMEM)
    vmem = pl.BlockSpec(memory_space=pltpu.VMEM)
    anywhere = pl.BlockSpec(memory_space=pltpu.HBM)
    whole = jax.ShapeDtypeStruct((tile_rows, tile_cols), jnp.float32)
    bf16, f32 = jnp.bfloat16, jnp.float32
    dma = pltpu.SemaphoreType.DMA
    scratch = [
        pltpu.VMEM((tile_rows, tile_cols), f32),
        pltpu.VMEM((tile_rows, tile_cols), f32),
        pltpu.VMEM(across.shape, bf16),
        pltpu.VMEM(down.shape, bf16),
        pltpu.VMEM((held, block, block), bf16),
        pltpu.VMEM((held, block, block), jnp.int32),
        pltpu.VMEM((CHUNKS, held, span, block), bf16),
        pltpu.VMEM((CHUNKS, held, span, block), bf16),
        pltpu.VMEM((held + 1, 3, block, block), f32),
        pltpu.VMEM((held + 1, 4, block, block), bf16),
        pltpu.VMEM((held + 1, block, block), f32),
        pltpu.VMEM((held + 1, block, block), f32),
        pltpu.SMEM((entries,), jnp.int32),
        pltpu.SMEM((entries,), jnp.int32),
        pltpu.VMEM((4, tile_rows, tile_cols + 2 * block), bf16),
        pltpu.VMEM((n, tile_rows, tile_cols), f32),
        pltpu.VMEM((n + 1, CHUNKS, BLOCK_ROWS, span, tile_cols), bf16),
        pltpu.VMEM((n + 1, PARTS, part, tile_cols), bf16),
        pltpu.VMEM((WIDE, part, tile_cols), f32),
        pltpu.VMEM((WIDE, part, tile_cols), f32),
        pltpu.VMEM((2, n, SPILL, tile_cols), bf16),
        pltpu.VMEM((2, n, SPILL, tile_cols), bf16),
        pltpu.VMEM((tile_rows, tile_cols), f32),
        pltpu.VMEM((tile_rows, tile_cols), f32),
        pltpu.VMEM((bands - 1, tile_rows, tile_cols), f32),
        dma((2,)),
        dma((CHUNKS, 2)),
        dma((1,)),
        dma((CHUNKS,)),
        dma((2,)),
        dma((n,)),
        dma((n + 1, CHUNKS)),
        dma((n,)),
        dma((n + 1, PARTS)),
        dma((1,)),
        dma((WIDE,)),
        dma((2,)),
        dma((2, n)),
        dma((bands - 1,)),
        dma((bands - 1, PARTS)),
        dma((2,)),
    ]
    held_bytes = sum(
        int(np.prod(x.shape)) * jnp.dtype(x.dtype).itemsize
        for x in scratch
        if x.memory_space == pltpu.VMEM
    )
    limit = min(held_bytes + (16 << 20), 60 * 1024 * 1024)
    coadd, detection = pl.pallas_call(
        functools.partial(coadd_kernel, n, strips, bands),
        out_shape=(whole, whole),
        in_specs=[smem] * 5 + [anywhere] * 4,
        out_specs=(pl.BlockSpec(memory_space=pl.ANY),) * 2,
        scratch_shapes=scratch,
        compiler_params=pltpu.CompilerParams(collective_id=0, has_side_effects=True, vmem_limit_bytes=limit),
        name="coadd",
    )(*[
        pltpu.with_memory_space_constraint(x, pltpu.HBM)
        for x in (
            routes[0, 0, :, 0], block_slot[0, 0], kernel_index[0, 0], inv_var[0, 0],
            coefficients.T, images[0, 0], mask_bits[0, 0], across, down,
        )
    ])
    coadd, detection = pl.pallas_call(
        hand_out_kernel,
        out_shape=(whole, whole),
        in_specs=[pl.BlockSpec(memory_space=pl.ANY)] * 2,
        out_specs=(anywhere,) * 2,
        scratch_shapes=[dma((2, HANDS))],
        compiler_params=pltpu.CompilerParams(vmem_limit_bytes=1 << 20),
        name="hand_out",
    )(coadd, detection)
    return coadd[None], detection


def solution(mesh):
    return jax.shard_map(
        functools.partial(local, dict(mesh.shape)),
        mesh=mesh,
        in_specs=(
            P(("patch", "band"), "tile", "exp", None, None),
            P(("patch", "band"), "tile", "exp", None, None),
            P(("patch", "band"), "tile", "exp"),
            P(("patch", "band"), "tile", "exp", None),
            P(("patch", "band"), "tile", "exp"),
            P(("patch", "band"), "tile", "exp"),
            P(),
        ),
        out_specs=(P(("patch", "band"), "tile", "exp"), P(("patch", "tile"), "exp")),
        check_vma=False,
    )
```
